512 devices in a mesh: fsdp: 16 (over x, y_lo, core), tm: 32 (over y_hi, z).
Axes of the slice: x: 4, y: 4 (y_hi: 2, y_lo: 2; y = y_hi * 2 + y_lo), z: 16, core: 2. Of those that a mesh axis runs over, the one named last changes fastest.
Arguments:
- tokens: bfloat16 [32, 32, 256, 1024], P('fsdp', 'tm'), may hold values from -6 to 6
- spatial_gain: float32 [1024], replicated, may hold values from 0.25 to 1.75
- spatial_qkv: bfloat16 [1024, 1536], P('fsdp'), may hold values from -16 to 16
- spatial_out: bfloat16 [512, 1024], P('fsdp'), may hold values from -0.25 to 0.25
- temporal_gain: float32 [1024], replicated, may hold values from 0.25 to 1.75
- temporal_qkv: bfloat16 [1024, 1536], P('fsdp'), may hold values from -16 to 16
- temporal_out: bfloat16 [512, 1024], P('fsdp'), may hold values from -0.25 to 0.25
Outputs:
- encoded: bfloat16 [32, 32, 256, 1024], P('fsdp', 'tm')
The draws below stay inside these ranges and needn't reach their ends.
All inputs are finite; a program needn't handle non-finite values.
Results may differ from the reference program's by a relative error of at most 0.0061.
Values may be sent and summed in bfloat16 or wider, within the bound.
No kernel may reach another device: no remote copies, remote signals or barrier semaphores. Data moves between devices by JAX's collectives and lax.ppermute only.
A program may use at most 64 MiB of HBM per device.

```python
import jax
import jax.numpy as jnp
from jax import lax

D = 1024
HEAD = 64
HEADS = 8
P_SIZE = 256
INNER = 512
CLIPS = 32
FRAMES = 32


def drawn_weight(key):
    column_count = 3 * INNER
    sample = jax.random.normal(key, (D, column_count), jnp.float32) * D ** (-0.5)
    return jnp.clip(sample, -16.0, 16.0)


def draw_spatial_qkv(key, part):
    return drawn_weight(jax.random.fold_in(key, 11)).astype(jnp.bfloat16)


def draw_temporal_qkv(key, part):
    return drawn_weight(jax.random.fold_in(key, 23)).astype(jnp.bfloat16)


def draw_tokens(key, part):
    sample = jax.random.normal(jax.random.fold_in(key, 5), (CLIPS, FRAMES, P_SIZE, D), jnp.float32)
    return jnp.clip(sample, -6.0, 6.0).astype(jnp.bfloat16)


def shard_levels(rng, dims, shards, least, high):
    level, own = 1.0, jax.random.fold_in(rng, 6)
    for dim, parts in shards:
        heights = jnp.exp(jax.random.uniform(jax.random.fold_in(own, dim), (parts,), jnp.float32, least / len(shards), high / len(shards)))
        level = level * jnp.repeat(heights, dims[dim] // parts).reshape([-1 if axis == dim else 1 for axis in range(len(dims))])
    return level


def bell_draw(key, shape, scale, reach, cuts=(), dtype=jnp.bfloat16):
    level = shard_levels(key, shape, cuts, -0.22, 0.18) if cuts else 1.0
    result = jax.random.normal(key, shape, jnp.float32) * scale * level
    return jnp.minimum(jnp.maximum(result, -reach), reach).astype(dtype)


def setup_inputs(seed: int = 0) -> dict:
    arg_keys = jax.random.split(jax.random.key(seed), 8)
    return {
        "tokens": draw_tokens(jax.random.fold_in(arg_keys[7], 71), 0),
        "spatial_gain": jnp.clip(1.0 + 0.15 * jax.random.normal(arg_keys[1], (D,), jnp.float32), 0.25, 1.75),
        "spatial_qkv": draw_spatial_qkv(jax.random.fold_in(arg_keys[7], 71), 0),
        "spatial_out": bell_draw(arg_keys[3], (INNER, D), INNER ** -0.5, 0.25, ((0, 16),)),
        "temporal_gain": jnp.clip(1.0 + 0.15 * jax.random.normal(arg_keys[4], (D,), jnp.float32), 0.25, 1.75),
        "temporal_qkv": draw_temporal_qkv(jax.random.fold_in(arg_keys[7], 71), 0),
        "temporal_out": bell_draw(arg_keys[6], (INNER, D), INNER ** -0.5, 0.25, ((0, 16),)),
    }


EPSILON = 1e-06

def norm_rows(source, norm_gain):
    values = source.astype(jnp.float32)
    centre = values - lax.optimization_barrier(jnp.mean(values, axis=-1, keepdims=True))
    spread = lax.optimization_barrier(jnp.mean(centre * centre, axis=-1, keepdims=True))
    return (centre * lax.rsqrt(spread + EPSILON) * norm_gain).astype(jnp.bfloat16)

def attention_core(projected):
    inner_width = projected.shape[-1] // 3
    lead_shape = projected.shape[:-1]
    queries = projected[..., :inner_width].reshape(lead_shape + (HEADS, HEAD))
    key_rows = projected[..., inner_width:2 * inner_width].reshape(lead_shape + (HEADS, HEAD))
    value_rows = projected[..., 2 * inner_width:].astype(jnp.bfloat16).reshape(lead_shape + (HEADS, HEAD))
    scores = jnp.einsum('blmhe,bkmhe->bmhlk', queries, key_rows, precision=lax.Precision.HIGHEST) * HEAD ** (-0.5)
    row_max = lax.optimization_barrier(jnp.max(scores, axis=-1, keepdims=True))
    exponent = jnp.exp(scores - row_max)
    weights = (exponent / lax.optimization_barrier(jnp.sum(exponent, axis=-1, keepdims=True))).astype(jnp.bfloat16)
    context = jnp.einsum('bmhlk,bkmhe->blmhe', weights.astype(jnp.float32), value_rows.astype(jnp.float32), precision=lax.Precision.HIGHEST)
    return context.astype(jnp.bfloat16).reshape(lead_shape + (inner_width,))

def reference(tokens, spatial_gain, spatial_qkv, spatial_out, temporal_gain, temporal_qkv, temporal_out):

    def encode_clip(clip_tokens):
        frame_count, place_count, feature_width = clip_tokens.shape
        normed = norm_rows(clip_tokens, spatial_gain).reshape(-1, feature_width)
        projected = jnp.dot(normed, spatial_qkv, preferred_element_type=jnp.float32)
        context = attention_core(projected.reshape(frame_count, place_count, 1, 3 * INNER)).reshape(-1, INNER)
        middle = (clip_tokens.astype(jnp.float32).reshape(-1, feature_width) + jnp.dot(context, spatial_out, preferred_element_type=jnp.float32)).astype(jnp.bfloat16)
        normed_t = norm_rows(middle, temporal_gain)
        projected_t = jnp.dot(normed_t, temporal_qkv, preferred_element_type=jnp.float32)
        context_t = attention_core(projected_t.reshape(1, frame_count, place_count, 3 * INNER)).reshape(-1, INNER)
        encoded = middle.astype(jnp.float32) + jnp.dot(context_t, temporal_out, preferred_element_type=jnp.float32)
        return encoded.astype(jnp.bfloat16).reshape(frame_count, place_count, feature_width)
    return lax.map(encode_clip, tokens)
```

```python
import functools

import jax
import jax.numpy as jnp
from jax import lax
from jax.experimental import pallas as pl
from jax.experimental.pallas import tpu as pltpu
from jax.sharding import PartitionSpec as P

HEAD = 64
HEADS = 8
INNER = 512
EPSILON = 1e-06
BF16, F32 = jnp.bfloat16, jnp.float32
GROUP = 8
PAIR = 2 * HEAD
ROWS = 256
MIB = 1 << 20


def norm_rows(values, gain):
    centre = values - jnp.mean(values, axis=-1, keepdims=True)
    spread = jnp.mean(centre * centre, axis=-1, keepdims=True)
    return centre * lax.rsqrt(spread + EPSILON) * gain


def attend(qkv, rows, same):
    low = lax.broadcasted_iota(jnp.int32, (ROWS, PAIR), 1) < HEAD
    outs = []
    for pair in range(HEADS // 2):
        queries = qkv[rows, pl.ds(pair * PAIR, PAIR)]
        keys = qkv[rows, pl.ds(INNER + pair * PAIR, PAIR)]
        values = qkv[rows, pl.ds(2 * INNER + pair * PAIR, PAIR)]
        halves = []
        for mine in (low, ~low):
            own = jnp.where(mine, queries, jnp.zeros_like(queries))
            scores = lax.dot_general(own, keys, (((1,), (1,)), ((), ())), preferred_element_type=F32)
            if same is not None:
                scores = jnp.where(same, scores, -1e30)
            exponent = jnp.exp(scores - jnp.max(scores, axis=-1, keepdims=True))
            weights = exponent * (1.0 / jnp.sum(exponent, axis=-1, keepdims=True))
            halves.append(jnp.dot(weights.astype(BF16), values, preferred_element_type=F32))
        outs.append(jnp.where(low, halves[0], halves[1]))
    return jnp.concatenate(outs, axis=1)


def out_weight(packed):
    parts, twice, width = packed.shape
    half = twice // 2
    left = packed[:, :half].reshape(parts * half, width)
    right = packed[:, half:].reshape(parts * half, width)
    return left, right


def start_weights(weights, qkv_weight, out_ref, sems):
    qkv_copy = pltpu.make_async_copy(weights.at[:, :, pl.ds(0, 3 * INNER)], qkv_weight, sems.at[0])
    out_copy = pltpu.make_async_copy(weights.at[:, :, pl.ds(3 * INNER, INNER)], out_ref, sems.at[1])
    return qkv_copy, out_copy


def project(normed, qkv_weight, store):
    depth = normed.shape[1]
    for piece in range(3 * INNER // 256):
        columns = pl.ds(piece * 256, 256)
        weight = qkv_weight[:, :, columns].reshape(depth, 256)
        product = jnp.dot(normed, weight, preferred_element_type=F32)
        if piece < INNER // 256:
            product = product * HEAD**-0.5
        store(columns, product)


def spatial_kernel(tokens, gain, weights, context, middle, qkv_weight, out_ref, qkv, sems):
    qkv_copy, out_copy = start_weights(weights, qkv_weight, out_ref, sems)
    qkv_copy.start()
    out_copy.start()
    normed = norm_rows(tokens[...].astype(F32), gain[...]).astype(BF16)
    qkv_copy.wait()

    def store(columns, product):
        qkv[:, columns] = product.astype(BF16)

    project(normed, qkv_weight, store)
    for clip in range(tokens.shape[0] // ROWS):
        rows = pl.ds(clip * ROWS, ROWS)
        context[rows, :] = attend(qkv, rows, None).astype(BF16)
    out_copy.wait()
    for half, weight in enumerate(out_weight(out_ref[...])):
        columns = pl.ds(half * INNER, INNER)
        added = jnp.dot(context[...], weight, preferred_element_type=F32)
        middle[:, columns] = (tokens[:, columns].astype(F32) + added).astype(BF16)


def temporal_kernel(frames, tokens, arrived, gain, first, second, context, qkv_weight, out_ref, qkv, sems):
    out_copy = pltpu.make_async_copy(first.at[:, :, pl.ds(3 * INNER, INNER)], out_ref, sems.at[0])
    qkv_copy = pltpu.make_async_copy(second.at[:, :, pl.ds(0, 3 * INNER)], qkv_weight, sems.at[1])
    out_copy.start()
    qkv_copy.start()
    depth = tokens.shape[1]
    out_copy.wait()
    added = jnp.concatenate(
        [jnp.dot(arrived[...], weight, preferred_element_type=F32) for weight in out_weight(out_ref[...])], axis=1
    )
    middle = (tokens[...].astype(F32) + added).astype(BF16).astype(F32)
    normed = norm_rows(middle, gain[...]).astype(BF16)
    qkv_copy.wait()
    places = tokens.shape[0] // frames

    def store(columns, product):
        split = product.reshape(frames, places, product.shape[1])
        for group in range(places // GROUP):
            own = split[:, group * GROUP : (group + 1) * GROUP].reshape(ROWS, product.shape[1])
            qkv[pl.ds(group * ROWS, ROWS), columns] = own.astype(BF16)

    project(normed, qkv_weight, store)
    place = lax.broadcasted_iota(jnp.int32, (ROWS, ROWS), 0) % GROUP
    same = place == lax.broadcasted_iota(jnp.int32, (ROWS, ROWS), 1) % GROUP
    outs = []
    for group in range(places // GROUP):
        out = attend(qkv, pl.ds(group * ROWS, ROWS), same)
        outs.append(out.reshape(frames, GROUP, INNER))
    context[...] = jnp.concatenate(outs, axis=1).reshape(tokens.shape[0], INNER).astype(BF16)


def kernel_call(body, ins, outs, members, operands, flops):
    depth = 2 * INNER
    rows = depth // members
    whole = pl.BlockSpec(memory_space=pltpu.VMEM)
    return pl.pallas_call(
        body,
        out_shape=outs,
        in_specs=[pl.BlockSpec(memory_space=pltpu.HBM) if far else whole for far in ins],
        out_specs=[whole] * len(outs),
        scratch_shapes=[
            pltpu.VMEM((members, rows, 3 * INNER), BF16),
            pltpu.VMEM((members, rows, INNER), BF16),
            pltpu.VMEM((2 * ROWS, 3 * INNER), BF16),
            pltpu.SemaphoreType.DMA((2,)),
        ],
        compiler_params=pltpu.CompilerParams(vmem_limit_bytes=40 * MIB),
        cost_estimate=pl.CostEstimate(flops=flops, bytes_accessed=8 * MIB, transcendentals=2 * MIB),
    )(*operands)


def side_by_side(qkv, out):
    return jnp.concatenate([qkv, jnp.concatenate([out[:, :INNER], out[:, INNER:]], axis=0)], axis=1)


def shards(tokens, spatial_gain, spatial_qkv, spatial_out, temporal_gain, temporal_qkv, temporal_out):
    clips, _, places, depth = tokens.shape
    frames = lax.axis_size("tm")
    members = lax.axis_size("fsdp")
    rows = clips * places
    block = rows // frames
    flat = tokens.reshape(rows, depth)

    def gathered(qkv, out):
        return lax.all_gather(side_by_side(qkv, out), "fsdp", axis=0, tiled=False)

    def exchanged(array):
        sent = array.reshape(frames, block, array.shape[1])
        return lax.all_to_all(sent, "tm", split_axis=0, concat_axis=0, tiled=True).reshape(array.shape)

    first = gathered(spatial_qkv, spatial_out)
    second = gathered(temporal_qkv, temporal_out)
    early = exchanged(flat)
    context, middle = kernel_call(
        spatial_kernel,
        [False, False, True],
        [jax.ShapeDtypeStruct((rows, INNER), BF16), jax.ShapeDtypeStruct((rows, depth), BF16)],
        members,
        (flat, spatial_gain.reshape(1, depth), first),
        4 * rows * depth * depth,
    )
    arrived = exchanged(context)
    (context_t,) = kernel_call(
        functools.partial(temporal_kernel, frames),
        [False, False, False, True, True],
        [jax.ShapeDtypeStruct((rows, INNER), BF16)],
        members,
        (early, arrived, temporal_gain.reshape(1, depth), first, second),
        4 * rows * depth * depth,
    )
    weight = jnp.concatenate(out_weight(second[:, :, 3 * INNER :]), axis=1)
    returned = exchanged(context_t)
    encoded = middle.astype(F32) + jnp.dot(returned, weight, preferred_element_type=F32)
    return encoded.astype(BF16).reshape(tokens.shape)


def solution(mesh):
    placed = (
        P("fsdp", "tm", None, None),
        P(),
        P("fsdp", None),
        P("fsdp", None),
        P(),
        P("fsdp", None),
        P("fsdp", None),
    )
    return jax.shard_map(
        shards, mesh=mesh, in_specs=placed, out_specs=P("fsdp", "tm", None, None), check_vma=False
    )
```

```python
import functools

import jax
import jax.numpy as jnp
from jax import lax
from jax.experimental import pallas as pl
from jax.experimental.pallas import tpu as pltpu
from jax.sharding import PartitionSpec as P

HEAD = 64
HEADS = 8
INNER = 512
EPSILON = 1e-06
BF16, F32 = jnp.bfloat16, jnp.float32
GROUP = 8
PAIR = 2 * HEAD
ROWS = 256
MIB = 1 << 20


def norm_rows(values, gain):
    centre = values - jnp.mean(values, axis=-1, keepdims=True)
    spread = jnp.mean(centre * centre, axis=-1, keepdims=True)
    return centre * lax.rsqrt(spread + EPSILON) * gain


def attend(qkv, rows, same):
    low = lax.broadcasted_iota(jnp.int32, (ROWS, PAIR), 1) < HEAD
    outs = []
    for pair in range(HEADS // 2):
        queries = qkv[rows, pl.ds(pair * PAIR, PAIR)]
        keys = qkv[rows, pl.ds(INNER + pair * PAIR, PAIR)]
        values = qkv[rows, pl.ds(2 * INNER + pair * PAIR, PAIR)]
        halves = []
        for mine in (low, ~low):
            own = jnp.where(mine, queries, jnp.zeros_like(queries))
            scores = lax.dot_general(own, keys, (((1,), (1,)), ((), ())), preferred_element_type=F32)
            if same is not None:
                scores = jnp.where(same, scores, -1e30)
            exponent = jnp.exp(scores - jnp.max(scores, axis=-1, keepdims=True))
            weights = exponent * (1.0 / jnp.sum(exponent, axis=-1, keepdims=True))
            halves.append(jnp.dot(weights.astype(BF16), values, preferred_element_type=F32))
        outs.append(jnp.where(low, halves[0], halves[1]))
    return jnp.concatenate(outs, axis=1)


def out_weight(packed):
    parts, twice, width = packed.shape
    half = twice // 2
    left = packed[:, :half].reshape(parts * half, width)
    right = packed[:, half:].reshape(parts * half, width)
    return left, right


def project(normed, weights, store):
    depth = normed.shape[1]
    for piece in range(3 * INNER // 256):
        columns = pl.ds(piece * 256, 256)
        product = jnp.dot(normed, weights[:, :, columns].reshape(depth, 256), preferred_element_type=F32)
        if piece < INNER // 256:
            product = product * HEAD**-0.5
        store(columns, product)


def pack_kernel(qkv, out, packed, sems):
    depth, width = qkv.shape
    half = out.shape[1] // 2
    copies = []
    for index in range(packed.shape[0]):
        target = packed.at[index]
        copies += [
            pltpu.make_async_copy(qkv, target.at[:, pl.ds(0, width)], sems.at[index, 0]),
            pltpu.make_async_copy(
                out.at[:, pl.ds(0, half)], target.at[pl.ds(0, depth // 2), pl.ds(width, half)], sems.at[index, 1]
            ),
            pltpu.make_async_copy(
                out.at[:, pl.ds(half, half)], target.at[pl.ds(depth // 2, depth // 2), pl.ds(width, half)], sems.at[index, 2]
            ),
        ]
    for copy in copies:
        copy.start()
    for copy in copies:
        copy.wait()


def packed_weights(qkv, out, copies):
    depth = qkv.shape[0]
    far = pl.BlockSpec(memory_space=pl.ANY)
    return pl.pallas_call(
        pack_kernel,
        out_shape=jax.ShapeDtypeStruct((copies, depth, qkv.shape[1] + INNER), BF16),
        in_specs=[far, far],
        out_specs=far,
        scratch_shapes=[pltpu.SemaphoreType.DMA((copies, 3))],
        cost_estimate=pl.CostEstimate(flops=0, bytes_accessed=copies * MIB // 2, transcendentals=0),
    )(qkv, out)


def place_kernel(here, mine, other, placed, sems):
    across, beside, core = here[0], here[1], here[2]
    copies = []
    for side, source in enumerate((mine, other)):
        for index in range(source.shape[0]):
            step = (0, -1, 1, 2)[index // 2]
            target = placed.at[(across + step + 4) % 4, (beside + index) % 2, (core + side) % 2]
            copies.append(pltpu.make_async_copy(source.at[index], target, sems.at[side, index]))
    for copy in copies:
        copy.start()
    for copy in copies:
        copy.wait()


def in_order(here, mine, other):
    parts, depth, width = mine.shape
    far = pl.BlockSpec(memory_space=pl.ANY)
    placed = pl.pallas_call(
        place_kernel,
        out_shape=jax.ShapeDtypeStruct((4, 2, 2, depth, width), BF16),
        in_specs=[pl.BlockSpec(memory_space=pltpu.SMEM), far, far],
        out_specs=far,
        scratch_shapes=[pltpu.SemaphoreType.DMA((2, parts))],
        cost_estimate=pl.CostEstimate(flops=0, bytes_accessed=8 * MIB, transcendentals=0),
    )(here, mine, other)
    return placed.reshape(2 * parts, depth, width)


def spatial_kernel(here, tokens, gain, mine, other, middle, weights, qkv, context, sems):
    core = here[2]
    copies = [
        pltpu.make_async_copy(mine, weights.at[:, core], sems.at[0]),
        pltpu.make_async_copy(other, weights.at[:, 1 - core], sems.at[1]),
    ]
    for copy in copies:
        copy.start()
    normed = norm_rows(tokens[...].astype(F32), gain[...]).astype(BF16)
    for copy in copies:
        copy.wait()
    parts, cores, depth, width = weights.shape
    whole = weights.reshape(parts * cores, depth, width)

    def store(columns, product):
        qkv[:, columns] = product.astype(BF16)

    project(normed, whole, store)
    for clip in range(tokens.shape[0] // ROWS):
        rows = pl.ds(clip * ROWS, ROWS)
        context[rows, :] = attend(qkv, rows, None).astype(BF16)
    for half, weight in enumerate(out_weight(whole[:, :, pl.ds(3 * INNER, INNER)])):
        columns = pl.ds(half * INNER, INNER)
        added = jnp.dot(context[...], weight, preferred_element_type=F32)
        middle[:, columns] = (tokens[:, columns].astype(F32) + added).astype(BF16)


def temporal_kernel(frames, middle, gain, placed, context, weights, qkv, sems):
    copy = pltpu.make_async_copy(placed.at[:, :, pl.ds(0, 3 * INNER)], weights, sems.at[0])
    copy.start()
    normed = norm_rows(middle[...].astype(F32), gain[...]).astype(BF16)
    copy.wait()
    places = middle.shape[0] // frames

    def store(columns, product):
        split = product.reshape(frames, places, product.shape[1])
        for group in range(places // GROUP):
            own = split[:, group * GROUP : (group + 1) * GROUP].reshape(ROWS, product.shape[1])
            qkv[pl.ds(group * ROWS, ROWS), columns] = own.astype(BF16)

    project(normed, weights, store)
    place = lax.broadcasted_iota(jnp.int32, (ROWS, ROWS), 0) % GROUP
    same = place == lax.broadcasted_iota(jnp.int32, (ROWS, ROWS), 1) % GROUP
    outs = []
    for group in range(places // GROUP):
        out = attend(qkv, pl.ds(group * ROWS, ROWS), same)
        outs.append(out.reshape(frames, GROUP, INNER))
    context[...] = jnp.concatenate(outs, axis=1).reshape(middle.shape[0], INNER).astype(BF16)


def kernel_call(body, kinds, out, scratch, operands):
    near = pl.BlockSpec(memory_space=pltpu.VMEM)
    specs = {"s": pl.BlockSpec(memory_space=pltpu.SMEM), "v": near, "h": pl.BlockSpec(memory_space=pl.ANY)}
    rows, depth = 2 * ROWS, 2 * INNER
    return pl.pallas_call(
        body,
        out_shape=out,
        in_specs=[specs[kind] for kind in kinds],
        out_specs=near,
        scratch_shapes=scratch,
        compiler_params=pltpu.CompilerParams(vmem_limit_bytes=57 * MIB),
        cost_estimate=pl.CostEstimate(flops=4 * rows * depth * depth, bytes_accessed=8 * MIB, transcendentals=2 * MIB),
    )(*operands)


def moved(array, change):
    pairs = []
    for index in range(lax.axis_size("fsdp")):
        x, yl, core = change(index // 4, index // 2 % 2, index % 2)
        pairs.append((index, (x % 4 * 2 + yl) * 2 + core))
    return lax.ppermute(array, "fsdp", pairs)


def other_core(array):
    return moved(array, lambda x, yl, core: (x, yl, 1 - core))


def gathered_by_hops(own):
    depth = own.shape[0]
    ahead = lambda x, yl, core: (x + 1, yl, core)
    back = lambda x, yl, core: (x + 3, yl, core)
    both = jnp.concatenate([own, moved(own, lambda x, yl, core: (x, 1 - yl, core))], axis=0)
    left, right = moved(both, ahead), moved(both, back)
    far = moved(left[:depth], ahead), moved(right[depth:], back)
    mine = jnp.concatenate([both, left, right, *far], axis=0).reshape(8, depth, own.shape[1])
    return mine, other_core(mine)


def shards(tokens, spatial_gain, spatial_qkv, spatial_out, temporal_gain, temporal_qkv, temporal_out):
    clips, _, places, depth = tokens.shape
    frames = lax.axis_size("tm")
    members = lax.axis_size("fsdp")
    parts = members // 2
    rows = clips * places
    block = rows // frames
    flat = tokens.reshape(rows, depth)
    index = lax.axis_index("fsdp")
    here = jnp.stack([index // 4, index // 2 % 2, index % 2]).astype(jnp.int32)
    cores = [list(range(core, members, 2)) for core in range(2)]
    width = 4 * INNER

    def exchanged(array):
        sent = array.reshape(frames, block, array.shape[1])
        return lax.all_to_all(sent, "tm", split_axis=0, concat_axis=0, tiled=True).reshape(array.shape)

    mine = lax.all_to_all(
        packed_weights(spatial_qkv, spatial_out, parts), "fsdp", 0, 0, axis_index_groups=cores, tiled=True
    )
    middle = kernel_call(
        spatial_kernel,
        "svvhh",
        jax.ShapeDtypeStruct((rows, depth), BF16),
        [
            pltpu.VMEM((parts, 2, depth // members, width), BF16),
            pltpu.VMEM((rows, 3 * INNER), BF16),
            pltpu.VMEM((rows, INNER), BF16),
            pltpu.SemaphoreType.DMA((2,)),
        ],
        (here, flat, spatial_gain.reshape(1, depth), mine, other_core(mine)),
    )
    arrived = exchanged(middle)
    own, _ = lax.optimization_barrier((packed_weights(temporal_qkv, temporal_out, 1)[0], middle[:8, :128]))
    placed = in_order(here, *gathered_by_hops(own))
    context = kernel_call(
        functools.partial(temporal_kernel, frames),
        "vvh",
        jax.ShapeDtypeStruct((rows, INNER), BF16),
        [
            pltpu.VMEM((members, depth // members, 3 * INNER), BF16),
            pltpu.VMEM((rows, 3 * INNER), BF16),
            pltpu.SemaphoreType.DMA((1,)),
        ],
        (arrived, temporal_gain.reshape(1, depth), placed),
    )
    weight = jnp.concatenate(out_weight(placed[:, :, 3 * INNER :]), axis=1)
    returned = exchanged(context)
    encoded = middle.astype(F32) + jnp.dot(returned, weight, preferred_element_type=F32)
    return encoded.astype(BF16).reshape(tokens.shape)


def solution(mesh):
    placed = (
        P("fsdp", "tm", None, None),
        P(),
        P("fsdp", None),
        P("fsdp", None),
        P(),
        P("fsdp", None),
        P("fsdp", None),
    )
    return jax.shard_map(
        shards, mesh=mesh, in_specs=placed, out_specs=P("fsdp", "tm", None, None), check_vma=False
    )
```

```python
import functools

import jax
import jax.numpy as jnp
from jax import lax
from jax.experimental import pallas as pl
from jax.experimental.pallas import tpu as pltpu
from jax.sharding import PartitionSpec as P

HEAD = 64
HEADS = 8
INNER = 512
EPSILON = 1e-06
BF16, F32 = jnp.bfloat16, jnp.float32
GROUP = 8
PAIR = 2 * HEAD
ROWS = 256
MIB = 1 << 20


def norm_rows(values, gain):
    centre = values - jnp.mean(values, axis=-1, keepdims=True)
    spread = jnp.mean(centre * centre, axis=-1, keepdims=True)
    return centre * lax.rsqrt(spread + EPSILON) * gain


def attend(qkv, rows, same):
    low = lax.broadcasted_iota(jnp.int32, (ROWS, PAIR), 1) < HEAD
    outs = []
    for pair in range(HEADS // 2):
        queries = qkv[rows, pl.ds(pair * PAIR, PAIR)]
        keys = qkv[rows, pl.ds(INNER + pair * PAIR, PAIR)]
        values = qkv[rows, pl.ds(2 * INNER + pair * PAIR, PAIR)]
        halves = []
        for mine in (low, ~low):
            own = jnp.where(mine, queries, jnp.zeros_like(queries))
            scores = lax.dot_general(own, keys, (((1,), (1,)), ((), ())), preferred_element_type=F32)
            if same is not None:
                scores = jnp.where(same, scores, -1e30)
            exponent = jnp.exp(scores - jnp.max(scores, axis=-1, keepdims=True))
            weights = exponent * (1.0 / jnp.sum(exponent, axis=-1, keepdims=True))
            halves.append(jnp.dot(weights.astype(BF16), values, preferred_element_type=F32))
        outs.append(jnp.where(low, halves[0], halves[1]))
    return jnp.concatenate(outs, axis=1)


def out_weight(packed):
    parts, twice, width = packed.shape
    half = twice // 2
    left = packed[:, :half].reshape(parts * half, width)
    right = packed[:, half:].reshape(parts * half, width)
    return left, right


def project(normed, weights, store):
    depth = normed.shape[1]
    for piece in range(3 * INNER // 256):
        columns = pl.ds(piece * 256, 256)
        product = jnp.dot(normed, weights[:, :, columns].reshape(depth, 256), preferred_element_type=F32)
        if piece < INNER // 256:
            product = product * HEAD**-0.5
        store(columns, product)


def pack_kernel(qkv, out, next_qkv, next_out, packed, next_packed):
    depth, width = qkv.shape
    half = out.shape[1] // 2

    def pack(qkv, out, target):
        target[:, pl.ds(0, width)] = qkv[...]
        target[pl.ds(0, depth // 2), pl.ds(width, half)] = out[:, pl.ds(0, half)]
        target[pl.ds(depth // 2, depth // 2), pl.ds(width, half)] = out[:, pl.ds(half, half)]

    for index in range(packed.shape[0]):
        pack(qkv, out, packed.at[index])
    pack(next_qkv, next_out, next_packed)


def packed_weights(qkv, out, next_qkv, next_out, copies):
    depth, width = qkv.shape[0], qkv.shape[1] + INNER
    near = pl.BlockSpec(memory_space=pltpu.VMEM)
    return pl.pallas_call(
        pack_kernel,
        out_shape=[
            jax.ShapeDtypeStruct((copies, depth, width), BF16),
            jax.ShapeDtypeStruct((depth, width), BF16),
        ],
        in_specs=[near] * 4,
        out_specs=[near] * 2,
        cost_estimate=pl.CostEstimate(flops=0, bytes_accessed=3 * MIB, transcendentals=0),
    )(qkv, out, next_qkv, next_out)


def fetches(here, mine, other, columns, placed, sems):
    across, beside, core = here[0], here[1], here[2]
    copies = []
    for side, source in enumerate((mine, other)):
        for index in range(source.shape[0]):
            step = (0, 3, 1, 2)[index // 2]
            row = ((across + step) % 4 * 2 + (beside + index) % 2) * 2 + (core + side) % 2
            copies.append(pltpu.make_async_copy(source.at[index, :, columns], placed.at[row], sems.at[side, index]))
    return copies


def place_kernel(here, mine, other, placed, sems):
    copies = fetches(here, mine, other, pl.ds(3 * INNER, INNER), placed, sems)
    for copy in copies:
        copy.start()
    for copy in copies:
        copy.wait()


def out_in_order(here, mine, other):
    parts, depth, _ = mine.shape
    far = pl.BlockSpec(memory_space=pl.ANY)
    return pl.pallas_call(
        place_kernel,
        out_shape=jax.ShapeDtypeStruct((2 * parts, depth, INNER), BF16),
        in_specs=[pl.BlockSpec(memory_space=pltpu.SMEM), far, far],
        out_specs=pl.BlockSpec(memory_space=pltpu.VMEM),
        scratch_shapes=[pltpu.SemaphoreType.DMA((2, parts))],
        cost_estimate=pl.CostEstimate(flops=0, bytes_accessed=2 * MIB, transcendentals=0),
    )(here, mine, other)


def spatial_kernel(here, tokens, gain, mine, other, middle, weights, qkv, context, sems):
    core = here[2]
    copies = [
        pltpu.make_async_copy(mine, weights.at[:, core], sems.at[0]),
        pltpu.make_async_copy(other, weights.at[:, 1 - core], sems.at[1]),
    ]
    for copy in copies:
        copy.start()
    normed = norm_rows(tokens[...].astype(F32), gain[...]).astype(BF16)
    for copy in copies:
        copy.wait()
    parts, cores, depth, width = weights.shape
    whole = weights.reshape(parts * cores, depth, width)

    def store(columns, product):
        qkv[:, columns] = product.astype(BF16)

    project(normed, whole, store)
    for clip in range(tokens.shape[0] // ROWS):
        rows = pl.ds(clip * ROWS, ROWS)
        context[rows, :] = attend(qkv, rows, None).astype(BF16)
    for half, weight in enumerate(out_weight(whole[:, :, pl.ds(3 * INNER, INNER)])):
        columns = pl.ds(half * INNER, INNER)
        added = jnp.dot(context[...], weight, preferred_element_type=F32)
        middle[:, columns] = (tokens[:, columns].astype(F32) + added).astype(BF16)


def temporal_kernel(frames, here, middle, gain, mine, other, context, weights, qkv, sems):
    copies = fetches(here, mine, other, pl.ds(0, 3 * INNER), weights, sems)
    for copy in copies:
        copy.start()
    normed = norm_rows(middle[...].astype(F32), gain[...]).astype(BF16)
    for copy in copies:
        copy.wait()
    places = middle.shape[0] // frames

    def store(columns, product):
        split = product.reshape(frames, places, product.shape[1])
        for group in range(places // GROUP):
            own = split[:, group * GROUP : (group + 1) * GROUP].reshape(ROWS, product.shape[1])
            qkv[pl.ds(group * ROWS, ROWS), columns] = own.astype(BF16)

    project(normed, weights, store)
    place = lax.broadcasted_iota(jnp.int32, (ROWS, ROWS), 0) % GROUP
    same = place == lax.broadcasted_iota(jnp.int32, (ROWS, ROWS), 1) % GROUP
    outs = []
    for group in range(places // GROUP):
        out = attend(qkv, pl.ds(group * ROWS, ROWS), same)
        outs.append(out.reshape(frames, GROUP, INNER))
    context[...] = jnp.concatenate(outs, axis=1).reshape(middle.shape[0], INNER).astype(BF16)


def kernel_call(body, kinds, out, scratch, operands):
    near = pl.BlockSpec(memory_space=pltpu.VMEM)
    specs = {"s": pl.BlockSpec(memory_space=pltpu.SMEM), "v": near, "h": pl.BlockSpec(memory_space=pl.ANY)}
    rows, depth = 2 * ROWS, 2 * INNER
    return pl.pallas_call(
        body,
        out_shape=out,
        in_specs=[specs[kind] for kind in kinds],
        out_specs=near,
        scratch_shapes=scratch,
        compiler_params=pltpu.CompilerParams(vmem_limit_bytes=40 * MIB),
        cost_estimate=pl.CostEstimate(flops=4 * rows * depth * depth, bytes_accessed=8 * MIB, transcendentals=2 * MIB),
    )(*operands)


def moved(array, change):
    pairs = []
    for index in range(lax.axis_size("fsdp")):
        x, yl, core = change(index // 4, index // 2 % 2, index % 2)
        pairs.append((index, (x % 4 * 2 + yl) * 2 + core))
    return lax.ppermute(array, "fsdp", pairs)


def other_core(array):
    return moved(array, lambda x, yl, core: (x, yl, 1 - core))


def gathered_by_hops(both):
    depth = both.shape[0] // 2
    ahead = lambda x, yl, core: (x + 1, yl, core)
    back = lambda x, yl, core: (x + 3, yl, core)
    left, right = moved(both, ahead), moved(both, back)
    far = moved(left[:depth], ahead), moved(right[depth:], back)
    mine = jnp.concatenate([both, left, right, *far], axis=0).reshape(8, depth, both.shape[1])
    return mine, other_core(mine)


def shards(tokens, spatial_gain, spatial_qkv, spatial_out, temporal_gain, temporal_qkv, temporal_out):
    clips, _, places, depth = tokens.shape
    frames = lax.axis_size("tm")
    members = lax.axis_size("fsdp")
    parts = members // 2
    rows = clips * places
    block = rows // frames
    flat = tokens.reshape(rows, depth)
    index = lax.axis_index("fsdp")
    here = jnp.stack([index // 4, index // 2 % 2, index % 2]).astype(jnp.int32)
    cores = [list(range(core, members, 2)) for core in range(2)]
    width = 4 * INNER

    def exchanged(array):
        sent = array.reshape(frames, block, array.shape[1])
        return lax.all_to_all(sent, "tm", split_axis=0, concat_axis=0, tiled=True).reshape(array.shape)

    packed, own = packed_weights(spatial_qkv, spatial_out, temporal_qkv, temporal_out, parts)
    mine = lax.all_to_all(packed, "fsdp", 0, 0, axis_index_groups=cores, tiled=True)
    own, mine = lax.optimization_barrier((own, mine))
    beside = moved(own, lambda x, yl, core: (x, 1 - yl, core))
    middle = kernel_call(
        spatial_kernel,
        "svvhh",
        jax.ShapeDtypeStruct((rows, depth), BF16),
        [
            pltpu.VMEM((parts, 2, depth // members, width), BF16),
            pltpu.VMEM((rows, 3 * INNER), BF16),
            pltpu.VMEM((rows, INNER), BF16),
            pltpu.SemaphoreType.DMA((2,)),
        ],
        (here, flat, spatial_gain.reshape(1, depth), mine, other_core(mine)),
    )
    own, beside, middle = lax.optimization_barrier((own, beside, middle))
    arrived = exchanged(middle)
    mine, other = gathered_by_hops(jnp.concatenate([own, beside], axis=0))
    context = kernel_call(
        functools.partial(temporal_kernel, frames),
        "svvhh",
        jax.ShapeDtypeStruct((rows, INNER), BF16),
        [
            pltpu.VMEM((members, depth // members, 3 * INNER), BF16),
            pltpu.VMEM((rows, 3 * INNER), BF16),
            pltpu.SemaphoreType.DMA((2, parts)),
        ],
        (here, arrived, temporal_gain.reshape(1, depth), mine, other),
    )
    weight = jnp.concatenate(out_weight(out_in_order(here, mine, other)), axis=1)
    returned = exchanged(context)
    encoded = middle.astype(F32) + jnp.dot(returned, weight, preferred_element_type=F32)
    return encoded.astype(BF16).reshape(tokens.shape)


def solution(mesh):
    placed = (
        P("fsdp", "tm", None, None),
        P(),
        P("fsdp", None),
        P("fsdp", None),
        P(),
        P("fsdp", None),
        P("fsdp", None),
    )
    return jax.shard_map(
        shards, mesh=mesh, in_specs=placed, out_specs=P("fsdp", "tm", None, None), check_vma=False
    )
```

```python
import functools

import jax
import jax.numpy as jnp
from jax import lax
from jax.experimental import pallas as pl
from jax.experimental.pallas import tpu as pltpu
from jax.sharding import PartitionSpec as P

HEAD = 64
HEADS = 8
INNER = 512
EPSILON = 1e-06
BF16, F32 = jnp.bfloat16, jnp.float32
GROUP = 8
PAIR = 2 * HEAD
ROWS = 256
MIB = 1 << 20


def norm_rows(values, gain):
    centre = values - jnp.mean(values, axis=-1, keepdims=True)
    spread = jnp.mean(centre * centre, axis=-1, keepdims=True)
    return centre * lax.rsqrt(spread + EPSILON) * gain


def attend(qkv, rows, same):
    low = lax.broadcasted_iota(jnp.int32, (ROWS, PAIR), 1) < HEAD
    outs = []
    for pair in range(HEADS // 2):
        queries = qkv[rows, pl.ds(pair * PAIR, PAIR)]
        keys = qkv[rows, pl.ds(INNER + pair * PAIR, PAIR)]
        values = qkv[rows, pl.ds(2 * INNER + pair * PAIR, PAIR)]
        halves = []
        for mine in (low, ~low):
            own = jnp.where(mine, queries, jnp.zeros_like(queries))
            scores = lax.dot_general(own, keys, (((1,), (1,)), ((), ())), preferred_element_type=F32)
            if same is not None:
                scores = jnp.where(same, scores, -1e30)
            exponent = jnp.exp(scores - jnp.max(scores, axis=-1, keepdims=True))
            weights = exponent * (1.0 / jnp.sum(exponent, axis=-1, keepdims=True))
            halves.append(jnp.dot(weights.astype(BF16), values, preferred_element_type=F32))
        outs.append(jnp.where(low, halves[0], halves[1]))
    return jnp.concatenate(outs, axis=1)


def project(product, store):
    for piece in range(3 * INNER // 256):
        columns = pl.ds(piece * 256, 256)
        value = product(columns)
        if piece < INNER // 256:
            value = value * HEAD**-0.5
        store(columns, value)


def pack_kernel(qkv, out, packed):
    depth, width = qkv.shape
    half = out.shape[1] // 2
    for index in range(packed.shape[0]):
        packed[index, :, pl.ds(0, width)] = qkv[...]
        packed[index, pl.ds(0, depth // 2), pl.ds(width, half)] = out[:, pl.ds(0, half)]
        packed[index, pl.ds(depth // 2, depth // 2), pl.ds(width, half)] = out[:, pl.ds(half, half)]


def run(copies):
    for copy in copies:
        copy.start()
    return copies


def wait(copies):
    for copy in copies:
        copy.wait()


def norm_kernel(here, tokens, gain, mine, other):
    normed = norm_rows(tokens[...].astype(F32), gain[...]).astype(BF16)
    depth, width = normed.shape[1], mine.shape[1]
    source = lax.broadcasted_iota(jnp.int32, (depth, width), 0)
    target = lax.broadcasted_iota(jnp.int32, (depth, width), 1)
    block = depth // 16
    first = target // block * (2 * block) + target % block
    for out, core in ((mine, here[2]), (other, 1 - here[2])):
        chosen = (source == first + core * block).astype(F32).astype(BF16)
        out[...] = jnp.dot(normed, chosen, preferred_element_type=F32).astype(BF16)


def half_kernel(normed, weights, partial):
    depth = normed.shape[1]
    for piece in range(partial.shape[1] // 256):
        columns = pl.ds(piece * 256, 256)
        partial[:, columns] = jnp.dot(
            normed[...], weights[:, :, columns].reshape(depth, 256), preferred_element_type=F32
        )


def spatial_kernel(here, tokens, partial, normed, mine, other, middle, out_ref, qkv, context, sems):
    core = here[2]
    outs = pl.ds(3 * INNER, INNER)
    copies = run(
        [
            pltpu.make_async_copy(mine.at[:, :, outs], out_ref.at[:, core], sems.at[0]),
            pltpu.make_async_copy(other.at[:, :, outs], out_ref.at[:, 1 - core], sems.at[1]),
        ]
    )
    depth = normed.shape[1]

    def product(columns):
        weight = other[:, :, columns].reshape(depth, 256)
        return partial[:, columns] + jnp.dot(normed[...], weight, preferred_element_type=F32)

    def store(columns, value):
        qkv[:, columns] = value.astype(BF16)

    project(product, store)
    for clip in range(tokens.shape[0] // ROWS):
        rows = pl.ds(clip * ROWS, ROWS)
        context[rows, :] = attend(qkv, rows, None).astype(BF16)
    wait(copies)
    parts, cores, twice, width = out_ref.shape
    half = twice // 2
    for side in range(2):
        columns = pl.ds(side * width, width)
        weight = out_ref[:, :, pl.ds(side * half, half)].reshape(parts * cores * half, width)
        added = jnp.dot(context[...], weight, preferred_element_type=F32)
        middle[:, columns] = (tokens[:, columns].astype(F32) + added).astype(BF16)


def fetches(here, mine, other, placed, sems):
    copies = []
    for side, source in enumerate((mine, other)):
        for beside in range(2):
            target = placed.at[:, (here[1] + beside) % 2, (here[2] + side) % 2]
            copies.append(pltpu.make_async_copy(source.at[beside], target, sems.at[side, beside]))
    return run(copies)


def place_kernel(here, mine, other, placed, sems):
    wait(fetches(here, mine, other, placed, sems))


def temporal_kernel(frames, middle, gain, placed, context, qkv):
    normed = norm_rows(middle[...].astype(F32), gain[...]).astype(BF16)
    rows, depth = middle.shape
    places = rows // frames

    def product(columns):
        weight = placed[:, :, :, :, columns].reshape(depth, 256)
        return jnp.dot(normed, weight, preferred_element_type=F32)

    def store(columns, value):
        split = value.reshape(frames, places, value.shape[1])
        for group in range(places // GROUP):
            own = split[:, group * GROUP : (group + 1) * GROUP].reshape(ROWS, value.shape[1])
            qkv[pl.ds(group * ROWS, ROWS), columns] = own.astype(BF16)

    project(product, store)
    place = lax.broadcasted_iota(jnp.int32, (ROWS, ROWS), 0) % GROUP
    same = place == lax.broadcasted_iota(jnp.int32, (ROWS, ROWS), 1) % GROUP
    outs = []
    for group in range(places // GROUP):
        out = attend(qkv, pl.ds(group * ROWS, ROWS), same)
        outs.append(out.reshape(frames, GROUP, INNER))
    context[...] = jnp.concatenate(outs, axis=1).reshape(rows, INNER).astype(BF16)


def kernel_call(body, kinds, out, operands, scratch=(), gflops=0, mib=4):
    near = pl.BlockSpec(memory_space=pltpu.VMEM)
    specs = {"s": pl.BlockSpec(memory_space=pltpu.SMEM), "v": near, "h": pl.BlockSpec(memory_space=pl.ANY)}
    return pl.pallas_call(
        body,
        out_shape=out,
        in_specs=[specs[kind] for kind in kinds],
        out_specs=jax.tree.map(lambda _: near, out),
        scratch_shapes=scratch,
        compiler_params=pltpu.CompilerParams(vmem_limit_bytes=24 * MIB),
        cost_estimate=pl.CostEstimate(flops=int(gflops * 1e9), bytes_accessed=mib * MIB, transcendentals=0),
    )(*operands)


def moved(array, change):
    pairs = []
    for index in range(lax.axis_size("fsdp")):
        x, yl, core = change(index // 4, index // 2 % 2, index % 2)
        pairs.append((index, (x * 2 + yl) * 2 + core))
    return lax.ppermute(array, "fsdp", pairs)


def other_core(array):
    return moved(array, lambda x, yl, core: (x, yl, 1 - core))


def along_x(shard):
    lines = [list(range(start, 16, 4)) for start in range(4)]
    own = lax.all_gather(shard, "fsdp", axis_index_groups=lines)
    mine = jnp.stack([own, moved(own, lambda x, yl, core: (x, 1 - yl, core))])
    return mine, other_core(mine)


def shards(tokens, spatial_gain, spatial_qkv, spatial_out, temporal_gain, temporal_qkv, temporal_out):
    clips, _, places, depth = tokens.shape
    frames = lax.axis_size("tm")
    members = lax.axis_size("fsdp")
    parts, part = members // 2, depth // members
    rows = clips * places
    block = rows // frames
    flat = tokens.reshape(rows, depth)
    index = lax.axis_index("fsdp")
    here = jnp.stack([index // 4, index // 2 % 2, index % 2]).astype(jnp.int32)
    cores = [list(range(core, members, 2)) for core in range(2)]
    shape = jax.ShapeDtypeStruct

    def exchanged(array):
        sent = array.reshape(frames, block, array.shape[1])
        return lax.all_to_all(sent, "tm", split_axis=0, concat_axis=0, tiled=True).reshape(array.shape)

    def in_order(shard):
        return kernel_call(
            place_kernel,
            "shh",
            shape((4, 2, 2, *shard.shape), BF16),
            (here, *along_x(shard)),
            [pltpu.SemaphoreType.DMA((2, 2))],
        )

    packed = kernel_call(pack_kernel, "vv", shape((parts, part, 4 * INNER), BF16), (spatial_qkv, spatial_out))
    mine = lax.all_to_all(packed, "fsdp", 0, 0, axis_index_groups=cores, tiled=True)
    normed, normed_other = kernel_call(
        norm_kernel,
        "svv",
        [shape((rows, depth // 2), BF16)] * 2,
        (here, flat, spatial_gain.reshape(1, depth)),
        gflops=2,
    )
    mine, normed, normed_other = lax.optimization_barrier((mine, normed, normed_other))
    partial = kernel_call(half_kernel, "vv", shape((rows, 3 * INNER), F32), (normed, mine), gflops=1)
    middle = kernel_call(
        spatial_kernel,
        "svvvvv",
        shape((rows, depth), BF16),
        (here, flat, partial, normed_other, mine, other_core(mine)),
        [
            pltpu.VMEM((parts, 2, part, INNER), BF16),
            pltpu.VMEM((rows, 3 * INNER), BF16),
            pltpu.VMEM((rows, INNER), BF16),
            pltpu.SemaphoreType.DMA((2,)),
        ],
        gflops=3,
    )
    shard, middle = lax.optimization_barrier((temporal_qkv, middle))
    arrived = exchanged(middle)
    context = kernel_call(
        functools.partial(temporal_kernel, frames),
        "vvv",
        shape((rows, INNER), BF16),
        (arrived, temporal_gain.reshape(1, depth), in_order(shard)),
        [pltpu.VMEM((rows, 3 * INNER), BF16)],
        gflops=4,
    )
    shard, context = lax.optimization_barrier((temporal_out, context))
    returned = exchanged(context)
    weight = in_order(shard).reshape(INNER, depth)
    encoded = middle.astype(F32) + jnp.dot(returned, weight, preferred_element_type=F32)
    return encoded.astype(BF16).reshape(tokens.shape)


def solution(mesh):
    placed = (
        P("fsdp", "tm", None, None),
        P(),
        P("fsdp", None),
        P("fsdp", None),
        P(),
        P("fsdp", None),
        P("fsdp", None),
    )
    return jax.shard_map(
        shards, mesh=mesh, in_specs=placed, out_specs=P("fsdp", "tm", None, None), check_vma=False
    )
```

```python
import functools

import jax
import jax.numpy as jnp
from jax import lax
from jax.experimental import pallas as pl
from jax.experimental.pallas import tpu as pltpu
from jax.sharding import PartitionSpec as P

HEAD = 64
HEADS = 8
INNER = 512
EPSILON = 1e-06
BF16, F32 = jnp.bfloat16, jnp.float32
GROUP = 8
PAIR = 2 * HEAD
ROWS = 256
MIB = 1 << 20


def norm_rows(values, gain):
    centre = values - jnp.mean(values, axis=-1, keepdims=True)
    spread = jnp.mean(centre * centre, axis=-1, keepdims=True)
    return centre * lax.rsqrt(spread + EPSILON) * gain


def attend(qkv, rows, same):
    low = lax.broadcasted_iota(jnp.int32, (ROWS, PAIR), 1) < HEAD
    outs = []
    for pair in range(HEADS // 2):
        queries = qkv[rows, pl.ds(pair * PAIR, PAIR)]
        keys = qkv[rows, pl.ds(INNER + pair * PAIR, PAIR)]
        values = qkv[rows, pl.ds(2 * INNER + pair * PAIR, PAIR)]
        halves = []
        for mine in (low, ~low):
            own = jnp.where(mine, queries, jnp.zeros_like(queries))
            scores = lax.dot_general(own, keys, (((1,), (1,)), ((), ())), preferred_element_type=F32)
            if same is not None:
                scores = jnp.where(same, scores, -1e30)
            exponent = jnp.exp(scores - jnp.max(scores, axis=-1, keepdims=True))
            weights = exponent * (1.0 / jnp.sum(exponent, axis=-1, keepdims=True))
            halves.append(jnp.dot(weights.astype(BF16), values, preferred_element_type=F32))
        outs.append(jnp.where(low, halves[0], halves[1]))
    return jnp.concatenate(outs, axis=1)


def project(product, store):
    for piece in range(3 * INNER // 256):
        columns = pl.ds(piece * 256, 256)
        value = product(columns)
        if piece < INNER // 256:
            value = value * HEAD**-0.5
        store(columns, value)


def run(copies):
    for copy in copies:
        copy.start()
    return copies


def wait(copies):
    for copy in copies:
        copy.wait()


def norm_kernel(here, tokens, gain, normed):
    values = norm_rows(tokens[...].astype(F32), gain[...]).astype(BF16)
    sides, _, width = normed.shape
    depth = values.shape[1]
    part = width // 4
    source = lax.broadcasted_iota(jnp.int32, (depth, width), 0)
    target = lax.broadcasted_iota(jnp.int32, (depth, width), 1)
    first = target // part * (4 * part) + target % part
    for side in range(sides):
        yl, core = (here[1] + side // 2) % 2, (here[2] + side % 2) % 2
        chosen = (source == first + (yl * 2 + core) * part).astype(F32).astype(BF16)
        normed[side] = jnp.dot(values, chosen, preferred_element_type=F32).astype(BF16)


def half_product(normed, side, weights, columns):
    width = normed.shape[2]
    return sum(
        jnp.dot(
            normed[side + index], weight[:, :, columns].reshape(width, 256), preferred_element_type=F32
        )
        for index, weight in enumerate(weights)
    )


def half_kernel(normed, mine, other, partial):
    for piece in range(partial.shape[1] // 256):
        columns = pl.ds(piece * 256, 256)
        partial[:, columns] = half_product(normed, 0, (mine, other), columns)


def spatial_kernel(partial, normed, mine, other, context, qkv):
    def product(columns):
        return partial[:, columns] + half_product(normed, 2, (mine, other), columns)

    def store(columns, value):
        qkv[:, columns] = value.astype(BF16)

    project(product, store)
    for clip in range(context.shape[0] // ROWS):
        rows = pl.ds(clip * ROWS, ROWS)
        context[rows, :] = attend(qkv, rows, None).astype(BF16)


def place_kernel(here, *refs):
    pieces, placed, sems = refs[:-2], refs[-2], refs[-1]
    copies = []
    for side, piece in enumerate(pieces):
        target = placed.at[:, (here[1] + side // 2) % 2, (here[2] + side % 2) % 2]
        copies.append(pltpu.make_async_copy(piece, target, sems.at[side]))
    wait(run(copies))


def middle_kernel(tokens, context, weight, middle):
    added = jnp.dot(context[...], weight[...], preferred_element_type=F32)
    middle[...] = (tokens[...].astype(F32) + added).astype(BF16)


def temporal_kernel(frames, tokens, arrived, out_weight, gain, placed, context, qkv):
    added = jnp.dot(arrived[...], out_weight[...], preferred_element_type=F32)
    middle = (tokens[...].astype(F32) + added).astype(BF16)
    normed = norm_rows(middle.astype(F32), gain[...]).astype(BF16)
    rows, depth = middle.shape
    places = rows // frames

    def product(columns):
        weight = placed[:, :, :, :, columns].reshape(depth, 256)
        return jnp.dot(normed, weight, preferred_element_type=F32)

    def store(columns, value):
        split = value.reshape(frames, places, value.shape[1])
        for group in range(places // GROUP):
            own = split[:, group * GROUP : (group + 1) * GROUP].reshape(ROWS, value.shape[1])
            qkv[pl.ds(group * ROWS, ROWS), columns] = own.astype(BF16)

    project(product, store)
    place = lax.broadcasted_iota(jnp.int32, (ROWS, ROWS), 0) % GROUP
    same = place == lax.broadcasted_iota(jnp.int32, (ROWS, ROWS), 1) % GROUP
    outs = []
    for group in range(places // GROUP):
        out = attend(qkv, pl.ds(group * ROWS, ROWS), same)
        outs.append(out.reshape(frames, GROUP, INNER))
    context[...] = jnp.concatenate(outs, axis=1).reshape(rows, INNER).astype(BF16)


def kernel_call(body, kinds, out, operands, scratch=(), gflops=0, mib=4):
    near = pl.BlockSpec(memory_space=pltpu.VMEM)
    specs = {"s": pl.BlockSpec(memory_space=pltpu.SMEM), "v": near, "h": pl.BlockSpec(memory_space=pl.ANY)}
    return pl.pallas_call(
        body,
        out_shape=out,
        in_specs=[specs[kind] for kind in kinds],
        out_specs=jax.tree.map(lambda _: near, out),
        scratch_shapes=scratch,
        compiler_params=pltpu.CompilerParams(vmem_limit_bytes=24 * MIB),
        cost_estimate=pl.CostEstimate(flops=int(gflops * 1e9), bytes_accessed=mib * MIB, transcendentals=0),
    )(*operands)


def moved(array, change):
    pairs = []
    for index in range(lax.axis_size("fsdp")):
        x, yl, core = change(index // 4, index // 2 % 2, index % 2)
        pairs.append((index, (x * 2 + yl) * 2 + core))
    return lax.ppermute(array, "fsdp", pairs)


def other_core(array):
    return moved(array, lambda x, yl, core: (x, yl, 1 - core))


def other_yl(array):
    return moved(array, lambda x, yl, core: (x, 1 - yl, core))


def along_x(shard):
    lines = [list(range(start, 16, 4)) for start in range(4)]
    return lax.all_gather(shard, "fsdp", axis_index_groups=lines)


def after(array, *others):
    return lax.optimization_barrier((array, *others))[0]


def shards(tokens, spatial_gain, spatial_qkv, spatial_out, temporal_gain, temporal_qkv, temporal_out):
    clips, _, places, depth = tokens.shape
    frames = lax.axis_size("tm")
    members = lax.axis_size("fsdp")
    rows = clips * places
    block = rows // frames
    flat = tokens.reshape(rows, depth)
    index = lax.axis_index("fsdp")
    here = jnp.stack([index // 4, index // 2 % 2, index % 2]).astype(jnp.int32)
    shape = jax.ShapeDtypeStruct

    def exchanged(array):
        sent = array.reshape(frames, block, array.shape[1])
        return lax.all_to_all(sent, "tm", split_axis=0, concat_axis=0, tiled=True).reshape(array.shape)

    def in_order(*pieces):
        part, width = pieces[0].shape[1:]
        return kernel_call(
            place_kernel,
            "s" + "h" * 4,
            shape((4, 2, 2, part, width), BF16),
            (here, *pieces),
            [pltpu.SemaphoreType.DMA((4,))],
        )

    early = exchanged(flat)
    normed = kernel_call(
        norm_kernel, "svv", shape((4, rows, depth // 4), BF16), (here, flat, spatial_gain.reshape(1, depth)), gflops=2
    )
    own = along_x(spatial_qkv)
    beside = other_yl(own)
    own_t = along_x(after(temporal_qkv, own))
    partial = kernel_call(
        half_kernel, "vvv", shape((rows, 3 * INNER), F32), (normed, own, other_core(own)), gflops=1
    )
    beside, own_t, partial = lax.optimization_barrier((beside, own_t, partial))
    beside_t = other_yl(own_t)
    context = kernel_call(
        spatial_kernel,
        "vvvv",
        shape((rows, INNER), BF16),
        (partial, normed, beside, other_core(beside)),
        [pltpu.VMEM((rows, 3 * INNER), BF16)],
        gflops=3,
    )
    shard, context, early, beside_t = lax.optimization_barrier((spatial_out, context, early, beside_t))
    arrived = exchanged(context)
    placed = in_order(own_t, other_core(own_t), beside_t, other_core(beside_t))
    own_o = along_x(shard)
    beside_o = other_yl(own_o)
    swapped = other_core(jnp.stack([own_o, beside_o]))
    out_weight = in_order(own_o, swapped[0], beside_o, swapped[1]).reshape(INNER, depth)
    context_t = kernel_call(
        functools.partial(temporal_kernel, frames),
        "vvvvv",
        shape((rows, INNER), BF16),
        (early, arrived, out_weight, temporal_gain.reshape(1, depth), placed),
        [pltpu.VMEM((rows, 3 * INNER), BF16)],
        gflops=4,
    )
    shard, context, context_t = lax.optimization_barrier((temporal_out, context, context_t))
    returned = exchanged(context_t)
    own_o = along_x(shard)
    beside_o = other_yl(own_o)
    swapped = other_core(jnp.stack([own_o, beside_o]))
    weight = in_order(own_o, swapped[0], beside_o, swapped[1]).reshape(INNER, depth)
    middle = kernel_call(middle_kernel, "vvv", shape((rows, depth), BF16), (flat, context, out_weight), gflops=1)
    encoded = middle.astype(F32) + jnp.dot(returned, weight, preferred_element_type=F32)
    return encoded.astype(BF16).reshape(tokens.shape)


def solution(mesh):
    placed = (
        P("fsdp", "tm", None, None),
        P(),
        P("fsdp", None),
        P("fsdp", None),
        P(),
        P("fsdp", None),
        P("fsdp", None),
    )
    return jax.shard_map(
        shards, mesh=mesh, in_specs=placed, out_specs=P("fsdp", "tm", None, None), check_vma=False
    )
```

```python
import functools

import jax
import jax.numpy as jnp
from jax import lax
from jax.experimental import pallas as pl
from jax.experimental.pallas import tpu as pltpu
from jax.sharding import PartitionSpec as P

HEAD = 64
HEADS = 8
INNER = 512
EPSILON = 1e-06
BF16, F32 = jnp.bfloat16, jnp.float32
GROUP = 8
PAIR = 2 * HEAD
ROWS = 256
MIB = 1 << 20


def norm_rows(values, gain):
    centre = values - jnp.mean(values, axis=-1, keepdims=True)
    spread = jnp.mean(centre * centre, axis=-1, keepdims=True)
    return centre * lax.rsqrt(spread + EPSILON) * gain


def attend(qkv, rows, same):
    low = lax.broadcasted_iota(jnp.int32, (ROWS, PAIR), 1) < HEAD
    outs = []
    for pair in range(HEADS // 2):
        queries = qkv[rows, pl.ds(pair * PAIR, PAIR)]
        keys = qkv[rows, pl.ds(INNER + pair * PAIR, PAIR)]
        values = qkv[rows, pl.ds(2 * INNER + pair * PAIR, PAIR)]
        halves = []
        for mine in (low, ~low):
            own = jnp.where(mine, queries, jnp.zeros_like(queries))
            scores = lax.dot_general(own, keys, (((1,), (1,)), ((), ())), preferred_element_type=F32)
            if same is not None:
                scores = jnp.where(same, scores, -1e30)
            exponent = jnp.exp(scores - jnp.max(scores, axis=-1, keepdims=True))
            weights = exponent * (1.0 / jnp.sum(exponent, axis=-1, keepdims=True))
            halves.append(jnp.dot(weights.astype(BF16), values, preferred_element_type=F32))
        outs.append(jnp.where(low, halves[0], halves[1]))
    return jnp.concatenate(outs, axis=1)


def project(product, store):
    for piece in range(3 * INNER // 256):
        columns = pl.ds(piece * 256, 256)
        value = product(columns)
        if piece < INNER // 256:
            value = value * HEAD**-0.5
        store(columns, value)


def run(copies):
    for copy in copies:
        copy.start()
    return copies


def wait(copies):
    for copy in copies:
        copy.wait()


def norm_kernel(here, tokens, gain, normed):
    values = norm_rows(tokens[...].astype(F32), gain[...]).astype(BF16)
    sides, _, width = normed.shape
    depth = values.shape[1]
    part = width // 4
    source = lax.broadcasted_iota(jnp.int32, (depth, width), 0)
    target = lax.broadcasted_iota(jnp.int32, (depth, width), 1)
    first = target // part * (4 * part) + target % part
    for side in range(sides):
        yl, core = (here[1] + side // 2) % 2, (here[2] + side % 2) % 2
        chosen = (source == first + (yl * 2 + core) * part).astype(F32).astype(BF16)
        normed[side] = jnp.dot(values, chosen, preferred_element_type=F32).astype(BF16)


def half_product(normed, side, weights, columns):
    width = normed.shape[2]
    return sum(
        jnp.dot(
            normed[side + index], weight[:, :, columns].reshape(width, 256), preferred_element_type=F32
        )
        for index, weight in enumerate(weights)
    )


def half_kernel(normed, mine, other, partial):
    for piece in range(partial.shape[1] // 256):
        columns = pl.ds(piece * 256, 256)
        partial[:, columns] = half_product(normed, 0, (mine, other), columns)


def spatial_kernel(partial, normed, mine, other, context, qkv):
    def product(columns):
        return partial[:, columns] + half_product(normed, 2, (mine, other), columns)

    def store(columns, value):
        qkv[:, columns] = value.astype(BF16)

    project(product, store)
    for clip in range(context.shape[0] // ROWS):
        rows = pl.ds(clip * ROWS, ROWS)
        context[rows, :] = attend(qkv, rows, None).astype(BF16)


def place_kernel(here, *refs):
    pieces, placed, sems = refs[:-2], refs[-2], refs[-1]
    copies = []
    for side, piece in enumerate(pieces):
        target = placed.at[:, (here[1] + side // 2) % 2, (here[2] + side % 2) % 2]
        copies.append(pltpu.make_async_copy(piece, target, sems.at[side]))
    wait(run(copies))


def middle_kernel(tokens, context, weight, middle):
    added = jnp.dot(context[...], weight[...], preferred_element_type=F32)
    middle[...] = (tokens[...].astype(F32) + added).astype(BF16)


def temporal_kernel(frames, tokens, arrived, out_weight, gain, placed, context, qkv):
    added = jnp.dot(arrived[...], out_weight[...], preferred_element_type=F32)
    middle = (tokens[...].astype(F32) + added).astype(BF16)
    normed = norm_rows(middle.astype(F32), gain[...]).astype(BF16)
    rows, depth = middle.shape
    places = rows // frames

    def product(columns):
        weight = placed[:, :, :, :, columns].reshape(depth, 256)
        return jnp.dot(normed, weight, preferred_element_type=F32)

    def store(columns, value):
        split = value.reshape(frames, places, value.shape[1])
        for group in range(places // GROUP):
            own = split[:, group * GROUP : (group + 1) * GROUP].reshape(ROWS, value.shape[1])
            qkv[pl.ds(group * ROWS, ROWS), columns] = own.astype(BF16)

    project(product, store)
    place = lax.broadcasted_iota(jnp.int32, (ROWS, ROWS), 0) % GROUP
    same = place == lax.broadcasted_iota(jnp.int32, (ROWS, ROWS), 1) % GROUP
    outs = []
    for group in range(places // GROUP):
        out = attend(qkv, pl.ds(group * ROWS, ROWS), same)
        outs.append(out.reshape(frames, GROUP, INNER))
    context[...] = jnp.concatenate(outs, axis=1).reshape(rows, INNER).astype(BF16)


def kernel_call(body, kinds, out, operands, scratch=(), gflops=0, mib=4):
    near = pl.BlockSpec(memory_space=pltpu.VMEM)
    specs = {"s": pl.BlockSpec(memory_space=pltpu.SMEM), "v": near, "h": pl.BlockSpec(memory_space=pl.ANY)}
    return pl.pallas_call(
        body,
        out_shape=out,
        in_specs=[specs[kind] for kind in kinds],
        out_specs=jax.tree.map(lambda _: near, out),
        scratch_shapes=scratch,
        compiler_params=pltpu.CompilerParams(vmem_limit_bytes=24 * MIB),
        cost_estimate=pl.CostEstimate(flops=int(gflops * 1e9), bytes_accessed=mib * MIB, transcendentals=0),
    )(*operands)


def moved(array, change):
    pairs = []
    for index in range(lax.axis_size("fsdp")):
        x, yl, core = change(index // 4, index // 2 % 2, index % 2)
        pairs.append((index, (x * 2 + yl) * 2 + core))
    return lax.ppermute(array, "fsdp", pairs)


def other_core(array):
    return moved(array, lambda x, yl, core: (x, yl, 1 - core))


def other_yl(array):
    members, frames = lax.axis_size("fsdp"), lax.axis_size("tm")
    half = array.shape[0] // 2
    pieces = []
    for turn, piece in enumerate((array[:half], array[half:])):
        pairs = []
        for source in range(members * frames):
            member, frame = source // frames, source % frames
            pairs.append((source, (member ^ 2) * frames + (frame + turn * frames // 2) % frames))
        pieces.append(lax.ppermute(piece, ("fsdp", "tm"), pairs))
    return jnp.concatenate(pieces, axis=0)


def along_x(shard):
    lines = [list(range(start, 16, 4)) for start in range(4)]
    return lax.all_gather(shard, "fsdp", axis_index_groups=lines)


def after(array, *others):
    return lax.optimization_barrier((array, *others))[0]


def shards(tokens, spatial_gain, spatial_qkv, spatial_out, temporal_gain, temporal_qkv, temporal_out):
    clips, _, places, depth = tokens.shape
    frames = lax.axis_size("tm")
    members = lax.axis_size("fsdp")
    rows = clips * places
    block = rows // frames
    flat = tokens.reshape(rows, depth)
    index = lax.axis_index("fsdp")
    here = jnp.stack([index // 4, index // 2 % 2, index % 2]).astype(jnp.int32)
    shape = jax.ShapeDtypeStruct

    def exchanged(array):
        sent = array.reshape(frames, block, array.shape[1])
        return lax.all_to_all(sent, "tm", split_axis=0, concat_axis=0, tiled=True).reshape(array.shape)

    def in_order(*pieces):
        part, width = pieces[0].shape[1:]
        return kernel_call(
            place_kernel,
            "s" + "h" * 4,
            shape((4, 2, 2, part, width), BF16),
            (here, *pieces),
            [pltpu.SemaphoreType.DMA((4,))],
        )

    early = exchanged(flat)
    normed = kernel_call(
        norm_kernel, "svv", shape((4, rows, depth // 4), BF16), (here, flat, spatial_gain.reshape(1, depth)), gflops=2
    )
    own = along_x(spatial_qkv)
    beside = other_yl(own)
    own_t = along_x(after(temporal_qkv, own))
    partial = kernel_call(
        half_kernel, "vvv", shape((rows, 3 * INNER), F32), (normed, own, other_core(own)), gflops=1
    )
    beside, own_t, partial = lax.optimization_barrier((beside, own_t, partial))
    beside_t = other_yl(own_t)
    context = kernel_call(
        spatial_kernel,
        "vvvv",
        shape((rows, INNER), BF16),
        (partial, normed, beside, other_core(beside)),
        [pltpu.VMEM((rows, 3 * INNER), BF16)],
        gflops=3,
    )
    shard, context, early = lax.optimization_barrier((spatial_out, context, early))
    arrived = exchanged(context)
    placed = in_order(own_t, other_core(own_t), beside_t, other_core(beside_t))
    own_o = along_x(shard)
    beside_o = other_yl(own_o)
    swapped = other_core(jnp.stack([own_o, beside_o]))
    out_weight = in_order(own_o, swapped[0], beside_o, swapped[1]).reshape(INNER, depth)
    context_t = kernel_call(
        functools.partial(temporal_kernel, frames),
        "vvvvv",
        shape((rows, INNER), BF16),
        (early, arrived, out_weight, temporal_gain.reshape(1, depth), placed),
        [pltpu.VMEM((rows, 3 * INNER), BF16)],
        gflops=4,
    )
    shard, context, context_t = lax.optimization_barrier((temporal_out, context, context_t))
    returned = exchanged(context_t)
    own_o = along_x(shard)
    beside_o = other_yl(own_o)
    swapped = other_core(jnp.stack([own_o, beside_o]))
    weight = in_order(own_o, swapped[0], beside_o, swapped[1]).reshape(INNER, depth)
    middle = kernel_call(middle_kernel, "vvv", shape((rows, depth), BF16), (flat, context, out_weight), gflops=1)
    encoded = middle.astype(F32) + jnp.dot(returned, weight, preferred_element_type=F32)
    return encoded.astype(BF16).reshape(tokens.shape)


def solution(mesh):
    placed = (
        P("fsdp", "tm", None, None),
        P(),
        P("fsdp", None),
        P("fsdp", None),
        P(),
        P("fsdp", None),
        P("fsdp", None),
    )
    return jax.shard_map(
        shards, mesh=mesh, in_specs=placed, out_specs=P("fsdp", "tm", None, None), check_vma=False
    )
```

```python
import functools

import jax
import jax.numpy as jnp
from jax import lax
from jax.experimental import pallas as pl
from jax.experimental.pallas import tpu as pltpu
from jax.sharding import PartitionSpec as P

HEAD = 64
HEADS = 8
INNER = 512
EPSILON = 1e-06
BF16, F32 = jnp.bfloat16, jnp.float32
GROUP = 8
PAIR = 2 * HEAD
ROWS = 256
MIB = 1 << 20


def norm_rows(values, gain):
    centre = values - jnp.mean(values, axis=-1, keepdims=True)
    spread = jnp.mean(centre * centre, axis=-1, keepdims=True)
    return centre * lax.rsqrt(spread + EPSILON) * gain


def attend(qkv, rows, same):
    low = lax.broadcasted_iota(jnp.int32, (ROWS, PAIR), 1) < HEAD
    outs = []
    for pair in range(HEADS // 2):
        queries = qkv[rows, pl.ds(pair * PAIR, PAIR)]
        keys = qkv[rows, pl.ds(INNER + pair * PAIR, PAIR)]
        values = qkv[rows, pl.ds(2 * INNER + pair * PAIR, PAIR)]
        halves = []
        for mine in (low, ~low):
            own = jnp.where(mine, queries, jnp.zeros_like(queries))
            scores = lax.dot_general(own, keys, (((1,), (1,)), ((), ())), preferred_element_type=F32)
            if same is not None:
                scores = jnp.where(same, scores, -1e30)
            exponent = jnp.exp(scores - jnp.max(scores, axis=-1, keepdims=True))
            weights = exponent * (1.0 / jnp.sum(exponent, axis=-1, keepdims=True))
            halves.append(jnp.dot(weights.astype(BF16), values, preferred_element_type=F32))
        outs.append(jnp.where(low, halves[0], halves[1]))
    return jnp.concatenate(outs, axis=1)


def project(product, store):
    for piece in range(3 * INNER // 256):
        columns = pl.ds(piece * 256, 256)
        value = product(columns)
        if piece < INNER // 256:
            value = value * HEAD**-0.5
        store(columns, value)


def pack_kernel(qkv, out, next_qkv, next_out, packed, next_packed, sems):
    depth, width = qkv.shape
    half = out.shape[1] // 2
    copies = []
    for index in range(packed.shape[0] + 1):
        if index < packed.shape[0]:
            pair, target = (qkv, out), packed.at[index]
        else:
            pair, target = (next_qkv, next_out), next_packed
        copies.append(pltpu.make_async_copy(pair[0], target.at[:, pl.ds(0, width)], sems.at[index, 0]))
        for side in range(2):
            rows, columns = pl.ds(side * depth // 2, depth // 2), pl.ds(side * half, half)
            place = target.at[rows, pl.ds(width, half)]
            copies.append(pltpu.make_async_copy(pair[1].at[:, columns], place, sems.at[index, 1 + side]))
    wait(run(copies))


def run(copies):
    for copy in copies:
        copy.start()
    return copies


def wait(copies):
    for copy in copies:
        copy.wait()


def norm_kernel(here, tokens, gain, mine, other):
    normed = norm_rows(tokens[...].astype(F32), gain[...]).astype(BF16)
    depth, width = normed.shape[1], mine.shape[1]
    source = lax.broadcasted_iota(jnp.int32, (depth, width), 0)
    target = lax.broadcasted_iota(jnp.int32, (depth, width), 1)
    block = depth // 16
    first = target // block * (2 * block) + target % block
    for out, core in ((mine, here[2]), (other, 1 - here[2])):
        chosen = (source == first + core * block).astype(F32).astype(BF16)
        out[...] = jnp.dot(normed, chosen, preferred_element_type=F32).astype(BF16)


def half_kernel(normed, weights, partial):
    depth = normed.shape[1]
    for piece in range(partial.shape[1] // 256):
        columns = pl.ds(piece * 256, 256)
        partial[:, columns] = jnp.dot(
            normed[...], weights[:, :, columns].reshape(depth, 256), preferred_element_type=F32
        )


def spatial_kernel(here, tokens, partial, normed, mine, other, middle, out_ref, qkv, context, sems):
    core = here[2]
    outs = pl.ds(3 * INNER, INNER)
    copies = run(
        [
            pltpu.make_async_copy(mine.at[:, :, outs], out_ref.at[:, core], sems.at[0]),
            pltpu.make_async_copy(other.at[:, :, outs], out_ref.at[:, 1 - core], sems.at[1]),
        ]
    )
    depth = normed.shape[1]

    def product(columns):
        weight = other[:, :, columns].reshape(depth, 256)
        return partial[:, columns] + jnp.dot(normed[...], weight, preferred_element_type=F32)

    def store(columns, value):
        qkv[:, columns] = value.astype(BF16)

    project(product, store)
    for clip in range(tokens.shape[0] // ROWS):
        rows = pl.ds(clip * ROWS, ROWS)
        context[rows, :] = attend(qkv, rows, None).astype(BF16)
    wait(copies)
    parts, cores, twice, width = out_ref.shape
    half = twice // 2
    for side in range(2):
        columns = pl.ds(side * width, width)
        weight = out_ref[:, :, pl.ds(side * half, half)].reshape(parts * cores * half, width)
        added = jnp.dot(context[...], weight, preferred_element_type=F32)
        middle[:, columns] = (tokens[:, columns].astype(F32) + added).astype(BF16)


def place_kernel(here, mine, other, qkv, out, sems):
    _, depth, width = qkv.shape
    half = out.shape[2] // 2
    copies = []
    for side, source in enumerate((mine, other)):
        for index in range(source.shape[0]):
            step = (0, 3, 1, 2)[index // 2]
            row = ((here[0] + step) % 4 * 2 + (here[1] + index) % 2) * 2 + (here[2] + side) % 2
            block = source.at[index]
            copies.append(pltpu.make_async_copy(block.at[:, pl.ds(0, width)], qkv.at[row], sems.at[side, index, 0]))
            for part in range(2):
                rows, columns = pl.ds(part * depth // 2, depth // 2), pl.ds(part * half, half)
                piece = block.at[rows, pl.ds(width, half)]
                copies.append(pltpu.make_async_copy(piece, out.at[row, :, columns], sems.at[side, index, 1 + part]))
    wait(run(copies))


def copy_kernel(source, target):
    target[...] = source[...]


def temporal_kernel(frames, middle, gain, placed, context, weights, qkv, sems):
    pieces = [pl.ds(piece * 256, 256) for piece in range(3 * INNER // 256)]
    copies = run(
        [
            pltpu.make_async_copy(placed.at[:, :, columns], weights.at[:, :, columns], sems.at[piece])
            for piece, columns in enumerate(pieces)
        ]
    )
    normed = norm_rows(middle[...].astype(F32), gain[...]).astype(BF16)
    rows, depth = middle.shape
    places = rows // frames

    def product(columns):
        copies[columns.start // 256].wait()
        weight = weights[:, :, columns].reshape(depth, 256)
        return jnp.dot(normed, weight, preferred_element_type=F32)

    def store(columns, value):
        split = value.reshape(frames, places, value.shape[1])
        for group in range(places // GROUP):
            own = split[:, group * GROUP : (group + 1) * GROUP].reshape(ROWS, value.shape[1])
            qkv[pl.ds(group * ROWS, ROWS), columns] = own.astype(BF16)

    project(product, store)
    place = lax.broadcasted_iota(jnp.int32, (ROWS, ROWS), 0) % GROUP
    same = place == lax.broadcasted_iota(jnp.int32, (ROWS, ROWS), 1) % GROUP
    outs = []
    for group in range(places // GROUP):
        out = attend(qkv, pl.ds(group * ROWS, ROWS), same)
        outs.append(out.reshape(frames, GROUP, INNER))
    context[...] = jnp.concatenate(outs, axis=1).reshape(rows, INNER).astype(BF16)


def kernel_call(body, kinds, out, operands, scratch=(), gflops=0, mib=4, room=24):
    near = pl.BlockSpec(memory_space=pltpu.VMEM)
    specs = {"s": pl.BlockSpec(memory_space=pltpu.SMEM), "v": near, "h": pl.BlockSpec(memory_space=pl.ANY)}
    return pl.pallas_call(
        body,
        out_shape=out,
        in_specs=[specs[kind] for kind in kinds],
        out_specs=jax.tree.map(lambda _: near, out),
        scratch_shapes=scratch,
        compiler_params=pltpu.CompilerParams(vmem_limit_bytes=room * MIB),
        cost_estimate=pl.CostEstimate(flops=int(gflops * 1e9), bytes_accessed=mib * MIB, transcendentals=0),
    )(*operands)


def moved(array, change):
    pairs = []
    for index in range(lax.axis_size("fsdp")):
        x, yl, core = change(index // 4, index // 2 % 2, index % 2)
        pairs.append((index, (x * 2 + yl) * 2 + core))
    return lax.ppermute(array, "fsdp", pairs)


def other_core(array):
    return moved(array, lambda x, yl, core: (x, yl, 1 - core))


def gathered_by_hops(both):
    depth = both.shape[0] // 2
    ahead = lambda x, yl, core: ((x + 1) % 4, yl, core)
    back = lambda x, yl, core: ((x + 3) % 4, yl, core)
    left, right = moved(both, ahead), moved(both, back)
    far = moved(left[:depth], ahead), moved(right[depth:], back)
    mine = jnp.concatenate([both, left, right, *far], axis=0).reshape(8, depth, both.shape[1])
    return mine, other_core(mine)


def shards(tokens, spatial_gain, spatial_qkv, spatial_out, temporal_gain, temporal_qkv, temporal_out):
    clips, _, places, depth = tokens.shape
    frames = lax.axis_size("tm")
    members = lax.axis_size("fsdp")
    parts, part = members // 2, depth // members
    rows = clips * places
    block = rows // frames
    flat = tokens.reshape(rows, depth)
    index = lax.axis_index("fsdp")
    here = jnp.stack([index // 4, index // 2 % 2, index % 2]).astype(jnp.int32)
    cores = [list(range(core, members, 2)) for core in range(2)]
    shape = jax.ShapeDtypeStruct

    def exchanged(array):
        sent = array.reshape(frames, block, array.shape[1])
        return lax.all_to_all(sent, "tm", split_axis=0, concat_axis=0, tiled=True).reshape(array.shape)

    packed, own = kernel_call(
        pack_kernel,
        "hhhh",
        [shape((parts, part, 4 * INNER), BF16), shape((part, 4 * INNER), BF16)],
        (spatial_qkv, spatial_out, temporal_qkv, temporal_out),
        [pltpu.SemaphoreType.DMA((parts + 1, 3))],
        room=60,
    )
    mine = lax.all_to_all(packed, "fsdp", 0, 0, axis_index_groups=cores, tiled=True)
    own, gain, mine = lax.optimization_barrier((own, spatial_gain, mine))
    beside = moved(own, lambda x, yl, core: (x, 1 - yl, core))
    normed, normed_other = kernel_call(
        norm_kernel,
        "svv",
        [shape((rows, depth // 2), BF16)] * 2,
        (here, flat, gain.reshape(1, depth)),
        gflops=2,
    )
    partial = kernel_call(half_kernel, "vv", shape((rows, 3 * INNER), F32), (normed, mine), gflops=1)
    middle = kernel_call(
        spatial_kernel,
        "svvvvv",
        shape((rows, depth), BF16),
        (here, flat, partial, normed_other, mine, other_core(mine)),
        [
            pltpu.VMEM((parts, 2, part, INNER), BF16),
            pltpu.VMEM((rows, 3 * INNER), BF16),
            pltpu.VMEM((rows, INNER), BF16),
            pltpu.SemaphoreType.DMA((2,)),
        ],
        gflops=3,
    )
    own, beside, middle = lax.optimization_barrier((own, beside, middle))
    arrived = exchanged(middle)
    placed, weight = kernel_call(
        place_kernel,
        "shh",
        [shape((members, part, 3 * INNER), BF16), shape((members, INNER // members, depth), BF16)],
        (here, *gathered_by_hops(jnp.concatenate([own, beside], axis=0))),
        [pltpu.SemaphoreType.DMA((2, parts, 3))],
        room=60,
    )
    context = kernel_call(
        functools.partial(temporal_kernel, frames),
        "vvh",
        shape((rows, INNER), BF16),
        (arrived, temporal_gain.reshape(1, depth), placed),
        [
            pltpu.VMEM((members, part, 3 * INNER), BF16),
            pltpu.VMEM((rows, 3 * INNER), BF16),
            pltpu.SemaphoreType.DMA((6,)),
        ],
        gflops=4,
        room=50,
    )
    middle, context = lax.optimization_barrier((middle, context))
    returned = exchanged(context)
    kept = kernel_call(copy_kernel, "v", shape((rows, depth), BF16), (middle,))
    encoded = kept.astype(F32) + jnp.dot(returned, weight.reshape(INNER, depth), preferred_element_type=F32)
    return encoded.astype(BF16).reshape(tokens.shape)


def solution(mesh):
    placed = (
        P("fsdp", "tm", None, None),
        P(),
        P("fsdp", None),
        P("fsdp", None),
        P(),
        P("fsdp", None),
        P("fsdp", None),
    )
    return jax.shard_map(
        shards, mesh=mesh, in_specs=placed, out_specs=P("fsdp", "tm", None, None), check_vma=False
    )
```

```python
import functools

import jax
import jax.numpy as jnp
from jax import lax
from jax.experimental import pallas as pl
from jax.experimental.pallas import tpu as pltpu
from jax.sharding import PartitionSpec as P

HEAD = 64
HEADS = 8
INNER = 512
EPSILON = 1e-06
BF16, F32 = jnp.bfloat16, jnp.float32
GROUP = 8
PAIR = 2 * HEAD
ROWS = 256
MIB = 1 << 20


def norm_rows(values, gain):
    centre = values - jnp.mean(values, axis=-1, keepdims=True)
    spread = jnp.mean(centre * centre, axis=-1, keepdims=True)
    return centre * lax.rsqrt(spread + EPSILON) * gain


def attend(qkv, rows, same):
    low = lax.broadcasted_iota(jnp.int32, (ROWS, PAIR), 1) < HEAD
    outs = []
    for pair in range(HEADS // 2):
        queries = qkv[rows, pl.ds(pair * PAIR, PAIR)]
        keys = qkv[rows, pl.ds(INNER + pair * PAIR, PAIR)]
        values = qkv[rows, pl.ds(2 * INNER + pair * PAIR, PAIR)]
        halves = []
        for mine in (low, ~low):
            own = jnp.where(mine, queries, jnp.zeros_like(queries))
            scores = lax.dot_general(own, keys, (((1,), (1,)), ((), ())), preferred_element_type=F32)
            if same is not None:
                scores = jnp.where(same, scores, -1e30)
            exponent = jnp.exp(scores - jnp.max(scores, axis=-1, keepdims=True))
            weights = exponent * (1.0 / jnp.sum(exponent, axis=-1, keepdims=True))
            halves.append(jnp.dot(weights.astype(BF16), values, preferred_element_type=F32))
        outs.append(jnp.where(low, halves[0], halves[1]))
    return jnp.concatenate(outs, axis=1)


def project(product, store):
    for piece in range(3 * INNER // 256):
        columns = pl.ds(piece * 256, 256)
        value = product(columns)
        if piece < INNER // 256:
            value = value * HEAD**-0.5
        store(columns, value)


def run(copies):
    for copy in copies:
        copy.start()
    return copies


def wait(copies):
    for copy in copies:
        copy.wait()


def pack_kernel(qkv, out, packed, sems):
    depth, width = qkv.shape
    half = out.shape[1] // 2
    copies = [pltpu.make_async_copy(qkv, packed.at[:, pl.ds(0, width)], sems.at[0])]
    for side in range(2):
        piece = out.at[:, pl.ds(side * half, half)]
        target = packed.at[pl.ds(side * depth // 2, depth // 2), pl.ds(width, half)]
        copies.append(pltpu.make_async_copy(piece, target, sems.at[1 + side]))
    wait(run(copies))


def place_kernel(here, *refs):
    pieces, placed, sems = refs[:-2], refs[-2], refs[-1]
    copies = []
    for side, piece in enumerate(pieces):
        target = placed.at[:, (here[1] + side // 2) % 2, (here[2] + side % 2) % 2]
        copies.append(pltpu.make_async_copy(piece, target, sems.at[side]))
    wait(run(copies))


def norm_kernel(tokens, gain, normed):
    normed[...] = norm_rows(tokens[...].astype(F32), gain[...]).astype(BF16)


def fetches(gathered, weights, sems):
    copies = []
    for piece in range(3 * INNER // 256):
        columns = pl.ds(piece * 256, 256)
        copies.append(pltpu.make_async_copy(gathered.at[:, :, columns], weights.at[:, :, columns], sems.at[piece]))
    return run(copies)


def multiplied(normed, weights, copies):
    def product(columns):
        copies[columns.start // 256].wait()
        weight = weights[:, :, columns].reshape(normed.shape[1], 256)
        return jnp.dot(normed, weight, preferred_element_type=F32)

    return product


def out_halves(packed):
    parts, twice, width = packed.shape
    half = twice // 2
    return [packed[:, side * half : (side + 1) * half].reshape(parts * half, width) for side in range(2)]


def spatial_kernel(normed, first, context, weights, qkv, sems):
    copies = fetches(first, weights, sems)

    def store(columns, value):
        qkv[:, columns] = value.astype(BF16)

    project(multiplied(normed[...], weights, copies), store)
    for clip in range(context.shape[0] // ROWS):
        rows = pl.ds(clip * ROWS, ROWS)
        context[rows, :] = attend(qkv, rows, None).astype(BF16)


def middle_kernel(tokens, context, second, middle, out_ref, sems):
    wait(run([pltpu.make_async_copy(second.at[:, :, pl.ds(3 * INNER, INNER)], out_ref, sems.at[0])]))
    for side, weight in enumerate(out_halves(out_ref[...])):
        columns = pl.ds(side * INNER, INNER)
        added = jnp.dot(context[...], weight, preferred_element_type=F32)
        middle[:, columns] = (tokens[:, columns].astype(F32) + added).astype(BF16)


def temporal_kernel(frames, tokens, arrived, gain, second, context, out_ref, weights, qkv, sems, out_sem):
    out_copy = run([pltpu.make_async_copy(second.at[:, :, pl.ds(3 * INNER, INNER)], out_ref, out_sem.at[0])])
    copies = fetches(second, weights, sems)
    wait(out_copy)
    added = [jnp.dot(arrived[...], weight, preferred_element_type=F32) for weight in out_halves(out_ref[...])]
    middle = (tokens[...].astype(F32) + jnp.concatenate(added, axis=1)).astype(BF16)
    normed = norm_rows(middle.astype(F32), gain[...]).astype(BF16)
    rows = middle.shape[0]
    places = rows // frames

    def store(columns, value):
        split = value.reshape(frames, places, value.shape[1])
        for group in range(places // GROUP):
            own = split[:, group * GROUP : (group + 1) * GROUP].reshape(ROWS, value.shape[1])
            qkv[pl.ds(group * ROWS, ROWS), columns] = own.astype(BF16)

    project(multiplied(normed, weights, copies), store)
    place = lax.broadcasted_iota(jnp.int32, (ROWS, ROWS), 0) % GROUP
    same = place == lax.broadcasted_iota(jnp.int32, (ROWS, ROWS), 1) % GROUP
    outs = []
    for group in range(places // GROUP):
        out = attend(qkv, pl.ds(group * ROWS, ROWS), same)
        outs.append(out.reshape(frames, GROUP, INNER))
    context[...] = jnp.concatenate(outs, axis=1).reshape(rows, INNER).astype(BF16)


def kernel_call(body, kinds, out, operands, scratch=(), gflops=0, mib=4, room=24):
    near = pl.BlockSpec(memory_space=pltpu.VMEM)
    specs = {"s": pl.BlockSpec(memory_space=pltpu.SMEM), "v": near, "h": pl.BlockSpec(memory_space=pl.ANY)}
    return pl.pallas_call(
        body,
        out_shape=out,
        in_specs=[specs[kind] for kind in kinds],
        out_specs=jax.tree.map(lambda _: near, out),
        scratch_shapes=scratch,
        compiler_params=pltpu.CompilerParams(vmem_limit_bytes=room * MIB),
        cost_estimate=pl.CostEstimate(flops=int(gflops * 1e9), bytes_accessed=mib * MIB, transcendentals=0),
    )(*operands)


def moved(array, change):
    pairs = []
    for index in range(lax.axis_size("fsdp")):
        x, yl, core = change(index // 4, index // 2 % 2, index % 2)
        pairs.append((index, (x * 2 + yl) * 2 + core))
    return lax.ppermute(array, "fsdp", pairs)


def along_x(shard):
    lines = [list(range(start, 16, 4)) for start in range(4)]
    return lax.all_gather(shard, "fsdp", axis_index_groups=lines)


def shards(tokens, spatial_gain, spatial_qkv, spatial_out, temporal_gain, temporal_qkv, temporal_out):
    clips, _, places, depth = tokens.shape
    frames = lax.axis_size("tm")
    members = lax.axis_size("fsdp")
    part = depth // members
    index = lax.axis_index("fsdp")
    here = jnp.stack([index // 4, index // 2 % 2, index % 2]).astype(jnp.int32)
    rows = clips * places
    block = rows // frames
    flat = tokens.reshape(rows, depth)
    shape = jax.ShapeDtypeStruct
    tied = lax.optimization_barrier
    qkv_room = [
        pltpu.VMEM((members, part, 3 * INNER), BF16),
        pltpu.VMEM((rows, 3 * INNER), BF16),
        pltpu.SemaphoreType.DMA((3 * INNER // 256,)),
    ]
    out_room = pltpu.VMEM((members, part, INNER), BF16)
    one = pltpu.SemaphoreType.DMA((1,))

    def exchanged(array):
        sent = array.reshape(frames, block, array.shape[1])
        return lax.all_to_all(sent, "tm", split_axis=0, concat_axis=0, tiled=True).reshape(array.shape)

    def gathered(shard):
        return lax.all_gather(shard, "fsdp", axis=0, tiled=False)

    first = gathered(spatial_qkv)
    early = exchanged(flat)
    normed = kernel_call(norm_kernel, "vv", shape((rows, depth), BF16), (flat, spatial_gain.reshape(1, depth)))
    packed = kernel_call(
        pack_kernel,
        "hh",
        shape((part, 4 * INNER), BF16),
        (temporal_qkv, spatial_out),
        [pltpu.SemaphoreType.DMA((3,))],
        room=60,
    )
    second = gathered(packed)
    own = along_x(temporal_out)
    beside = moved(own, lambda x, yl, core: (x, 1 - yl, core))
    swapped = moved(jnp.stack([own, beside]), lambda x, yl, core: (x, yl, 1 - core))
    third = kernel_call(
        place_kernel,
        "shhhh",
        shape((4, 2, 2, INNER // members, depth), BF16),
        (here, own, swapped[0], beside, swapped[1]),
        [pltpu.SemaphoreType.DMA((4,))],
    )
    context = kernel_call(
        spatial_kernel, "vh", shape((rows, INNER), BF16), (normed, first), qkv_room, gflops=3, room=50
    )
    context, early, third = tied((context, early, third))
    arrived = exchanged(context)
    context_t = kernel_call(
        functools.partial(temporal_kernel, frames),
        "vvvh",
        shape((rows, INNER), BF16),
        (early, arrived, temporal_gain.reshape(1, depth), second),
        [out_room, *qkv_room, one],
        gflops=4,
        room=50,
    )
    context, context_t = tied((context, context_t))
    returned = exchanged(context_t)
    middle = kernel_call(
        middle_kernel, "vvh", shape((rows, depth), BF16), (flat, context, second), [out_room, one], gflops=1
    )
    encoded = middle.astype(F32) + jnp.dot(returned, third.reshape(INNER, depth), preferred_element_type=F32)
    return encoded.astype(BF16).reshape(tokens.shape)


def solution(mesh):
    placed = (
        P("fsdp", "tm", None, None),
        P(),
        P("fsdp", None),
        P("fsdp", None),
        P(),
        P("fsdp", None),
        P("fsdp", None),
    )
    return jax.shard_map(
        shards, mesh=mesh, in_specs=placed, out_specs=P("fsdp", "tm", None, None), check_vma=False
    )
```

```python
import functools

import jax
import jax.numpy as jnp
from jax import lax
from jax.experimental import pallas as pl
from jax.experimental.pallas import tpu as pltpu
from jax.sharding import PartitionSpec as P

HEAD = 64
HEADS = 8
INNER = 512
EPSILON = 1e-06
BF16, F32 = jnp.bfloat16, jnp.float32
GROUP = 8
PAIR = 2 * HEAD
ROWS = 256
MIB = 1 << 20


def norm_rows(values, gain):
    centre = values - jnp.mean(values, axis=-1, keepdims=True)
    spread = jnp.mean(centre * centre, axis=-1, keepdims=True)
    return centre * lax.rsqrt(spread + EPSILON) * gain


def attend(qkv, rows, same):
    low = lax.broadcasted_iota(jnp.int32, (ROWS, PAIR), 1) < HEAD
    outs = []
    for pair in range(HEADS // 2):
        queries = qkv[rows, pl.ds(pair * PAIR, PAIR)]
        keys = qkv[rows, pl.ds(INNER + pair * PAIR, PAIR)]
        values = qkv[rows, pl.ds(2 * INNER + pair * PAIR, PAIR)]
        halves = []
        for mine in (low, ~low):
            own = jnp.where(mine, queries, jnp.zeros_like(queries))
            scores = lax.dot_general(own, keys, (((1,), (1,)), ((), ())), preferred_element_type=F32)
            if same is not None:
                scores = jnp.where(same, scores, -1e30)
            exponent = jnp.exp(scores - jnp.max(scores, axis=-1, keepdims=True))
            weights = exponent * (1.0 / jnp.sum(exponent, axis=-1, keepdims=True))
            halves.append(jnp.dot(weights.astype(BF16), values, preferred_element_type=F32))
        outs.append(jnp.where(low, halves[0], halves[1]))
    return jnp.concatenate(outs, axis=1)


def project(product, store):
    for piece in range(3 * INNER // 256):
        columns = pl.ds(piece * 256, 256)
        value = product(columns)
        if piece < INNER // 256:
            value = value * HEAD**-0.5
        store(columns, value)


def pack_kernel(qkv, out, packed):
    depth, width = qkv.shape
    half = out.shape[1] // 2
    for index in range(packed.shape[0]):
        packed[index, :, pl.ds(0, width)] = qkv[...]
        packed[index, pl.ds(0, depth // 2), pl.ds(width, half)] = out[:, pl.ds(0, half)]
        packed[index, pl.ds(depth // 2, depth // 2), pl.ds(width, half)] = out[:, pl.ds(half, half)]


def run(copies):
    for copy in copies:
        copy.start()
    return copies


def wait(copies):
    for copy in copies:
        copy.wait()


def norm_kernel(here, tokens, gain, mine, other):
    normed = norm_rows(tokens[...].astype(F32), gain[...]).astype(BF16)
    depth, width = normed.shape[1], mine.shape[1]
    source = lax.broadcasted_iota(jnp.int32, (depth, width), 0)
    target = lax.broadcasted_iota(jnp.int32, (depth, width), 1)
    block = depth // 16
    first = target // block * (2 * block) + target % block
    for out, core in ((mine, here[2]), (other, 1 - here[2])):
        chosen = (source == first + core * block).astype(F32).astype(BF16)
        out[...] = jnp.dot(normed, chosen, preferred_element_type=F32).astype(BF16)


def half_kernel(normed, weights, partial):
    depth = normed.shape[1]
    for piece in range(partial.shape[1] // 256):
        columns = pl.ds(piece * 256, 256)
        partial[:, columns] = jnp.dot(
            normed[...], weights[:, :, columns].reshape(depth, 256), preferred_element_type=F32
        )


def spatial_kernel(here, tokens, partial, normed, mine, other, middle, out_ref, qkv, context, sems):
    core = here[2]
    outs = pl.ds(3 * INNER, INNER)
    copies = run(
        [
            pltpu.make_async_copy(mine.at[:, :, outs], out_ref.at[:, core], sems.at[0]),
            pltpu.make_async_copy(other.at[:, :, outs], out_ref.at[:, 1 - core], sems.at[1]),
        ]
    )
    depth = normed.shape[1]

    def product(columns):
        weight = other[:, :, columns].reshape(depth, 256)
        return partial[:, columns] + jnp.dot(normed[...], weight, preferred_element_type=F32)

    def store(columns, value):
        qkv[:, columns] = value.astype(BF16)

    project(product, store)
    for clip in range(tokens.shape[0] // ROWS):
        rows = pl.ds(clip * ROWS, ROWS)
        context[rows, :] = attend(qkv, rows, None).astype(BF16)
    wait(copies)
    parts, cores, twice, width = out_ref.shape
    half = twice // 2
    for side in range(2):
        columns = pl.ds(side * width, width)
        weight = out_ref[:, :, pl.ds(side * half, half)].reshape(parts * cores * half, width)
        added = jnp.dot(context[...], weight, preferred_element_type=F32)
        middle[:, columns] = (tokens[:, columns].astype(F32) + added).astype(BF16)


def place_kernel(here, *refs):
    pieces, placed, sems = refs[:-2], refs[-2], refs[-1]
    copies = []
    for side, piece in enumerate(pieces):
        target = placed.at[:, (here[1] + side // 2) % 2, (here[2] + side % 2) % 2]
        copies.append(pltpu.make_async_copy(piece, target, sems.at[side]))
    wait(run(copies))


def copy_kernel(source, target):
    target[...] = source[...]


def temporal_kernel(frames, middle, gain, placed, context, qkv):
    normed = norm_rows(middle[...].astype(F32), gain[...]).astype(BF16)
    rows, depth = middle.shape
    places = rows // frames

    def product(columns):
        weight = placed[:, :, :, :, columns].reshape(depth, 256)
        return jnp.dot(normed, weight, preferred_element_type=F32)

    def store(columns, value):
        split = value.reshape(frames, places, value.shape[1])
        for group in range(places // GROUP):
            own = split[:, group * GROUP : (group + 1) * GROUP].reshape(ROWS, value.shape[1])
            qkv[pl.ds(group * ROWS, ROWS), columns] = own.astype(BF16)

    project(product, store)
    place = lax.broadcasted_iota(jnp.int32, (ROWS, ROWS), 0) % GROUP
    same = place == lax.broadcasted_iota(jnp.int32, (ROWS, ROWS), 1) % GROUP
    outs = []
    for group in range(places // GROUP):
        out = attend(qkv, pl.ds(group * ROWS, ROWS), same)
        outs.append(out.reshape(frames, GROUP, INNER))
    context[...] = jnp.concatenate(outs, axis=1).reshape(rows, INNER).astype(BF16)


def kernel_call(body, kinds, out, operands, scratch=(), gflops=0, mib=4, room=24):
    near = pl.BlockSpec(memory_space=pltpu.VMEM)
    specs = {"s": pl.BlockSpec(memory_space=pltpu.SMEM), "v": near, "h": pl.BlockSpec(memory_space=pl.ANY)}
    return pl.pallas_call(
        body,
        out_shape=out,
        in_specs=[specs[kind] for kind in kinds],
        out_specs=jax.tree.map(lambda _: near, out),
        scratch_shapes=scratch,
        compiler_params=pltpu.CompilerParams(vmem_limit_bytes=room * MIB),
        cost_estimate=pl.CostEstimate(flops=int(gflops * 1e9), bytes_accessed=mib * MIB, transcendentals=0),
    )(*operands)


def moved(array, change):
    pairs = []
    for index in range(lax.axis_size("fsdp")):
        x, yl, core = change(index // 4, index // 2 % 2, index % 2)
        pairs.append((index, (x * 2 + yl) * 2 + core))
    return lax.ppermute(array, "fsdp", pairs)


def other_core(array):
    return moved(array, lambda x, yl, core: (x, yl, 1 - core))


def other_yl(array):
    members, frames = lax.axis_size("fsdp"), lax.axis_size("tm")
    half = array.shape[0] // 2
    pieces = []
    for turn, piece in enumerate((array[:half], array[half:])):
        pairs = []
        for source in range(members * frames):
            member, frame = source // frames, source % frames
            pairs.append((source, (member ^ 2) * frames + (frame + turn * frames // 2) % frames))
        pieces.append(lax.ppermute(piece, ("fsdp", "tm"), pairs))
    return jnp.concatenate(pieces, axis=0)


def along_x(shard):
    lines = [list(range(start, 16, 4)) for start in range(4)]
    return lax.all_gather(shard, "fsdp", axis_index_groups=lines)


def shards(tokens, spatial_gain, spatial_qkv, spatial_out, temporal_gain, temporal_qkv, temporal_out):
    clips, _, places, depth = tokens.shape
    frames = lax.axis_size("tm")
    members = lax.axis_size("fsdp")
    parts, part = members // 2, depth // members
    rows = clips * places
    block = rows // frames
    flat = tokens.reshape(rows, depth)
    index = lax.axis_index("fsdp")
    here = jnp.stack([index // 4, index // 2 % 2, index % 2]).astype(jnp.int32)
    cores = [list(range(core, members, 2)) for core in range(2)]
    shape = jax.ShapeDtypeStruct

    def exchanged(array):
        sent = array.reshape(frames, block, array.shape[1])
        return lax.all_to_all(sent, "tm", split_axis=0, concat_axis=0, tiled=True).reshape(array.shape)

    def in_order(*pieces):
        return kernel_call(
            place_kernel,
            "s" + "h" * 4,
            shape((4, 2, 2, *pieces[0].shape[1:]), BF16),
            (here, *pieces),
            [pltpu.SemaphoreType.DMA((4,))],
        )

    packed = kernel_call(
        pack_kernel, "vv", shape((parts, part, 4 * INNER), BF16), (spatial_qkv, spatial_out), room=60
    )
    mine = lax.all_to_all(packed, "fsdp", 0, 0, axis_index_groups=cores, tiled=True)
    normed, normed_other = kernel_call(
        norm_kernel,
        "svv",
        [shape((rows, depth // 2), BF16)] * 2,
        (here, flat, spatial_gain.reshape(1, depth)),
        gflops=2,
    )
    partial = kernel_call(half_kernel, "vv", shape((rows, 3 * INNER), F32), (normed, mine), gflops=1)
    middle = kernel_call(
        spatial_kernel,
        "svvvvv",
        shape((rows, depth), BF16),
        (here, flat, partial, normed_other, mine, other_core(mine)),
        [
            pltpu.VMEM((parts, 2, part, INNER), BF16),
            pltpu.VMEM((rows, 3 * INNER), BF16),
            pltpu.VMEM((rows, INNER), BF16),
            pltpu.SemaphoreType.DMA((2,)),
        ],
        gflops=3,
    )
    shard, middle = lax.optimization_barrier((temporal_qkv, middle))
    arrived = exchanged(middle)
    own = along_x(shard)
    beside = other_yl(own)
    placed = in_order(own, other_core(own), beside, other_core(beside))
    context = kernel_call(
        functools.partial(temporal_kernel, frames),
        "vvv",
        shape((rows, INNER), BF16),
        (arrived, temporal_gain.reshape(1, depth), placed),
        [pltpu.VMEM((rows, 3 * INNER), BF16)],
        gflops=4,
    )
    shard, middle, context = lax.optimization_barrier((temporal_out, middle, context))
    returned = exchanged(context)
    own = along_x(shard)
    beside = moved(own, lambda x, yl, core: (x, 1 - yl, core))
    swapped = other_core(jnp.stack([own, beside]))
    weight = in_order(own, swapped[0], beside, swapped[1]).reshape(INNER, depth)
    kept = kernel_call(copy_kernel, "v", shape((rows, depth), BF16), (middle,))
    encoded = kept.astype(F32) + jnp.dot(returned, weight, preferred_element_type=F32)
    return encoded.astype(BF16).reshape(tokens.shape)


def solution(mesh):
    placed = (
        P("fsdp", "tm", None, None),
        P(),
        P("fsdp", None),
        P("fsdp", None),
        P(),
        P("fsdp", None),
        P("fsdp", None),
    )
    return jax.shard_map(
        shards, mesh=mesh, in_specs=placed, out_specs=P("fsdp", "tm", None, None), check_vma=False
    )
```

```python
import functools

import jax
import jax.numpy as jnp
from jax import lax
from jax.experimental import pallas as pl
from jax.experimental.pallas import tpu as pltpu
from jax.sharding import PartitionSpec as P

HEAD = 64
HEADS = 8
INNER = 512
EPSILON = 1e-06
BF16, F32 = jnp.bfloat16, jnp.float32
GROUP = 8
PAIR = 2 * HEAD
ROWS = 256
MIB = 1 << 20


def norm_rows(values, gain):
    centre = values - jnp.mean(values, axis=-1, keepdims=True)
    spread = jnp.mean(centre * centre, axis=-1, keepdims=True)
    return centre * lax.rsqrt(spread + EPSILON) * gain


def attend(qkv, rows, same):
    low = lax.broadcasted_iota(jnp.int32, (ROWS, PAIR), 1) < HEAD
    outs = []
    for pair in range(HEADS // 2):
        queries = qkv[rows, pl.ds(pair * PAIR, PAIR)]
        keys = qkv[rows, pl.ds(INNER + pair * PAIR, PAIR)]
        values = qkv[rows, pl.ds(2 * INNER + pair * PAIR, PAIR)]
        halves = []
        for mine in (low, ~low):
            own = jnp.where(mine, queries, jnp.zeros_like(queries))
            scores = lax.dot_general(own, keys, (((1,), (1,)), ((), ())), preferred_element_type=F32)
            if same is not None:
                scores = jnp.where(same, scores, -1e30)
            exponent = jnp.exp(scores - jnp.max(scores, axis=-1, keepdims=True))
            weights = exponent * (1.0 / jnp.sum(exponent, axis=-1, keepdims=True))
            halves.append(jnp.dot(weights.astype(BF16), values, preferred_element_type=F32))
        outs.append(jnp.where(low, halves[0], halves[1]))
    return jnp.concatenate(outs, axis=1)


def project(product, store):
    for piece in range(3 * INNER // 256):
        columns = pl.ds(piece * 256, 256)
        value = product(columns)
        if piece < INNER // 256:
            value = value * HEAD**-0.5
        store(columns, value)


def pack_kernel(qkv, out, packed):
    depth, width = qkv.shape
    half = out.shape[1] // 2
    for index in range(packed.shape[0]):
        packed[index, :, pl.ds(0, width)] = qkv[...]
        packed[index, pl.ds(0, depth // 2), pl.ds(width, half)] = out[:, pl.ds(0, half)]
        packed[index, pl.ds(depth // 2, depth // 2), pl.ds(width, half)] = out[:, pl.ds(half, half)]


def run(copies):
    for copy in copies:
        copy.start()
    return copies


def wait(copies):
    for copy in copies:
        copy.wait()


def norm_kernel(here, tokens, gain, mine, other):
    normed = norm_rows(tokens[...].astype(F32), gain[...]).astype(BF16)
    depth, width = normed.shape[1], mine.shape[1]
    source = lax.broadcasted_iota(jnp.int32, (depth, width), 0)
    target = lax.broadcasted_iota(jnp.int32, (depth, width), 1)
    block = depth // 16
    first = target // block * (2 * block) + target % block
    for out, core in ((mine, here[2]), (other, 1 - here[2])):
        chosen = (source == first + core * block).astype(F32).astype(BF16)
        out[...] = jnp.dot(normed, chosen, preferred_element_type=F32).astype(BF16)


def half_kernel(normed, weights, partial):
    depth = normed.shape[1]
    for piece in range(partial.shape[1] // 256):
        columns = pl.ds(piece * 256, 256)
        partial[:, columns] = jnp.dot(
            normed[...], weights[:, :, columns].reshape(depth, 256), preferred_element_type=F32
        )


def spatial_kernel(here, tokens, partial, normed, mine, other, middle, out_ref, qkv, context, sems):
    core = here[2]
    outs = pl.ds(3 * INNER, INNER)
    copies = run(
        [
            pltpu.make_async_copy(mine.at[:, :, outs], out_ref.at[:, core], sems.at[0]),
            pltpu.make_async_copy(other.at[:, :, outs], out_ref.at[:, 1 - core], sems.at[1]),
        ]
    )
    depth = normed.shape[1]

    def product(columns):
        weight = other[:, :, columns].reshape(depth, 256)
        return partial[:, columns] + jnp.dot(normed[...], weight, preferred_element_type=F32)

    def store(columns, value):
        qkv[:, columns] = value.astype(BF16)

    project(product, store)
    for clip in range(tokens.shape[0] // ROWS):
        rows = pl.ds(clip * ROWS, ROWS)
        context[rows, :] = attend(qkv, rows, None).astype(BF16)
    wait(copies)
    parts, cores, twice, width = out_ref.shape
    half = twice // 2
    for side in range(2):
        columns = pl.ds(side * width, width)
        weight = out_ref[:, :, pl.ds(side * half, half)].reshape(parts * cores * half, width)
        added = jnp.dot(context[...], weight, preferred_element_type=F32)
        middle[:, columns] = (tokens[:, columns].astype(F32) + added).astype(BF16)


def place_kernel(here, *refs):
    pieces, placed, sems = refs[:-2], refs[-2], refs[-1]
    copies = []
    for side, piece in enumerate(pieces):
        target = placed.at[:, (here[1] + side // 2) % 2, (here[2] + side % 2) % 2]
        copies.append(pltpu.make_async_copy(piece, target, sems.at[side]))
    wait(run(copies))


def copy_kernel(source, target):
    target[...] = source[...]


def temporal_kernel(frames, middle, gain, placed, context, qkv):
    normed = norm_rows(middle[...].astype(F32), gain[...]).astype(BF16)
    rows, depth = middle.shape
    places = rows // frames

    def product(columns):
        weight = placed[:, :, :, :, columns].reshape(depth, 256)
        return jnp.dot(normed, weight, preferred_element_type=F32)

    def store(columns, value):
        split = value.reshape(frames, places, value.shape[1])
        for group in range(places // GROUP):
            own = split[:, group * GROUP : (group + 1) * GROUP].reshape(ROWS, value.shape[1])
            qkv[pl.ds(group * ROWS, ROWS), columns] = own.astype(BF16)

    project(product, store)
    place = lax.broadcasted_iota(jnp.int32, (ROWS, ROWS), 0) % GROUP
    same = place == lax.broadcasted_iota(jnp.int32, (ROWS, ROWS), 1) % GROUP
    outs = []
    for group in range(places // GROUP):
        out = attend(qkv, pl.ds(group * ROWS, ROWS), same)
        outs.append(out.reshape(frames, GROUP, INNER))
    context[...] = jnp.concatenate(outs, axis=1).reshape(rows, INNER).astype(BF16)


def kernel_call(body, kinds, out, operands, scratch=(), gflops=0, mib=4, room=24):
    near = pl.BlockSpec(memory_space=pltpu.VMEM)
    specs = {"s": pl.BlockSpec(memory_space=pltpu.SMEM), "v": near, "h": pl.BlockSpec(memory_space=pl.ANY)}
    return pl.pallas_call(
        body,
        out_shape=out,
        in_specs=[specs[kind] for kind in kinds],
        out_specs=jax.tree.map(lambda _: near, out),
        scratch_shapes=scratch,
        compiler_params=pltpu.CompilerParams(vmem_limit_bytes=room * MIB),
        cost_estimate=pl.CostEstimate(flops=int(gflops * 1e9), bytes_accessed=mib * MIB, transcendentals=0),
    )(*operands)


def moved(array, change):
    pairs = []
    for index in range(lax.axis_size("fsdp")):
        x, yl, core = change(index // 4, index // 2 % 2, index % 2)
        pairs.append((index, (x * 2 + yl) * 2 + core))
    return lax.ppermute(array, "fsdp", pairs)


def other_core(array):
    return moved(array, lambda x, yl, core: (x, yl, 1 - core))


def other_yl(array):
    members, frames = lax.axis_size("fsdp"), lax.axis_size("tm")
    half = array.shape[0] // 2
    pieces = []
    for turn, piece in enumerate((array[:half], array[half:])):
        pairs = []
        for source in range(members * frames):
            member, frame = source // frames, source % frames
            pairs.append((source, (member ^ 2) * frames + (frame + turn * frames // 2) % frames))
        pieces.append(lax.ppermute(piece, ("fsdp", "tm"), pairs))
    return jnp.concatenate(pieces, axis=0)


def along_x(shard):
    lines = [list(range(start, 16, 4)) for start in range(4)]
    return lax.all_gather(shard, "fsdp", axis_index_groups=lines)


def after(array, other):
    return lax.optimization_barrier((array, other))[0]


def shards(tokens, spatial_gain, spatial_qkv, spatial_out, temporal_gain, temporal_qkv, temporal_out):
    clips, _, places, depth = tokens.shape
    frames = lax.axis_size("tm")
    members = lax.axis_size("fsdp")
    parts, part = members // 2, depth // members
    rows = clips * places
    block = rows // frames
    flat = tokens.reshape(rows, depth)
    index = lax.axis_index("fsdp")
    here = jnp.stack([index // 4, index // 2 % 2, index % 2]).astype(jnp.int32)
    cores = [list(range(core, members, 2)) for core in range(2)]
    shape = jax.ShapeDtypeStruct

    def exchanged(array):
        sent = array.reshape(frames, block, array.shape[1])
        return lax.all_to_all(sent, "tm", split_axis=0, concat_axis=0, tiled=True).reshape(array.shape)

    def in_order(*pieces):
        return kernel_call(
            place_kernel,
            "s" + "h" * 4,
            shape((4, 2, 2, *pieces[0].shape[1:]), BF16),
            (here, *pieces),
            [pltpu.SemaphoreType.DMA((4,))],
        )

    packed = kernel_call(
        pack_kernel, "vv", shape((parts, part, 4 * INNER), BF16), (spatial_qkv, spatial_out), room=60
    )
    mine = lax.all_to_all(packed, "fsdp", 0, 0, axis_index_groups=cores, tiled=True)
    normed, normed_other = kernel_call(
        norm_kernel,
        "svv",
        [shape((rows, depth // 2), BF16)] * 2,
        (here, flat, spatial_gain.reshape(1, depth)),
        gflops=2,
        room=24,
    )
    partial = kernel_call(half_kernel, "vv", shape((rows, 3 * INNER), F32), (normed, mine), gflops=1, room=24)
    middle = kernel_call(
        spatial_kernel,
        "svvvvv",
        shape((rows, depth), BF16),
        (here, flat, partial, normed_other, mine, other_core(mine)),
        [
            pltpu.VMEM((parts, 2, part, INNER), BF16),
            pltpu.VMEM((rows, 3 * INNER), BF16),
            pltpu.VMEM((rows, INNER), BF16),
            pltpu.SemaphoreType.DMA((2,)),
        ],
        gflops=3,
        room=24,
    )
    shard, middle = lax.optimization_barrier((temporal_qkv, middle))
    arrived = exchanged(middle)
    own = along_x(shard)
    own_o = along_x(after(temporal_out, own))
    beside = other_yl(own)
    placed = in_order(own, other_core(own), beside, other_core(beside))
    arrived, own_o = lax.optimization_barrier((arrived, own_o))
    context = kernel_call(
        functools.partial(temporal_kernel, frames),
        "vvv",
        shape((rows, INNER), BF16),
        (arrived, temporal_gain.reshape(1, depth), placed),
        [pltpu.VMEM((rows, 3 * INNER), BF16)],
        gflops=4,
    )
    own, middle, context = lax.optimization_barrier((own_o, middle, context))
    returned = exchanged(context)
    beside = moved(own, lambda x, yl, core: (x, 1 - yl, core))
    swapped = other_core(jnp.stack([own, beside]))
    weight = in_order(own, swapped[0], beside, swapped[1]).reshape(INNER, depth)
    kept = kernel_call(copy_kernel, "v", shape((rows, depth), BF16), (middle,))
    encoded = kept.astype(F32) + jnp.dot(returned, weight, preferred_element_type=F32)
    return encoded.astype(BF16).reshape(tokens.shape)


def solution(mesh):
    placed = (
        P("fsdp", "tm", None, None),
        P(),
        P("fsdp", None),
        P("fsdp", None),
        P(),
        P("fsdp", None),
        P("fsdp", None),
    )
    return jax.shard_map(
        shards, mesh=mesh, in_specs=placed, out_specs=P("fsdp", "tm", None, None), check_vma=False
    )
```

```python
import functools

import jax
import jax.numpy as jnp
from jax import lax
from jax.experimental import pallas as pl
from jax.experimental.pallas import tpu as pltpu
from jax.sharding import PartitionSpec as P

HEAD = 64
HEADS = 8
INNER = 512
EPSILON = 1e-06
BF16, F32 = jnp.bfloat16, jnp.float32
GROUP = 8
PAIR = 2 * HEAD
ROWS = 256
MIB = 1 << 20


def norm_rows(values, gain):
    centre = values - jnp.mean(values, axis=-1, keepdims=True)
    spread = jnp.mean(centre * centre, axis=-1, keepdims=True)
    return centre * lax.rsqrt(spread + EPSILON) * gain


def attend(qkv, rows, same):
    low = lax.broadcasted_iota(jnp.int32, (ROWS, PAIR), 1) < HEAD
    outs = []
    for pair in range(HEADS // 2):
        queries = qkv[rows, pl.ds(pair * PAIR, PAIR)]
        keys = qkv[rows, pl.ds(INNER + pair * PAIR, PAIR)]
        values = qkv[rows, pl.ds(2 * INNER + pair * PAIR, PAIR)]
        halves = []
        for mine in (low, ~low):
            own = jnp.where(mine, queries, jnp.zeros_like(queries))
            scores = lax.dot_general(own, keys, (((1,), (1,)), ((), ())), preferred_element_type=F32)
            if same is not None:
                scores = jnp.where(same, scores, -1e30)
            exponent = jnp.exp(scores - jnp.max(scores, axis=-1, keepdims=True))
            weights = exponent * (1.0 / jnp.sum(exponent, axis=-1, keepdims=True))
            halves.append(jnp.dot(weights.astype(BF16), values, preferred_element_type=F32))
        outs.append(jnp.where(low, halves[0], halves[1]))
    return jnp.concatenate(outs, axis=1)


def project(product, store):
    for piece in range(3 * INNER // 256):
        columns = pl.ds(piece * 256, 256)
        value = product(columns)
        if piece < INNER // 256:
            value = value * HEAD**-0.5
        store(columns, value)


def pack_kernel(qkv, out, packed):
    depth, width = qkv.shape
    half = out.shape[1] // 2
    for index in range(packed.shape[0]):
        packed[index, :, pl.ds(0, width)] = qkv[...]
        packed[index, pl.ds(0, depth // 2), pl.ds(width, half)] = out[:, pl.ds(0, half)]
        packed[index, pl.ds(depth // 2, depth // 2), pl.ds(width, half)] = out[:, pl.ds(half, half)]


def run(copies):
    for copy in copies:
        copy.start()
    return copies


def wait(copies):
    for copy in copies:
        copy.wait()


def norm_kernel(here, tokens, gain, mine, other):
    normed = norm_rows(tokens[...].astype(F32), gain[...]).astype(BF16)
    depth, width = normed.shape[1], mine.shape[1]
    source = lax.broadcasted_iota(jnp.int32, (depth, width), 0)
    target = lax.broadcasted_iota(jnp.int32, (depth, width), 1)
    block = depth // 16
    first = target // block * (2 * block) + target % block
    for out, core in ((mine, here[2]), (other, 1 - here[2])):
        chosen = (source == first + core * block).astype(F32).astype(BF16)
        out[...] = jnp.dot(normed, chosen, preferred_element_type=F32).astype(BF16)


def half_kernel(normed, weights, partial):
    depth = normed.shape[1]
    for piece in range(partial.shape[1] // 256):
        columns = pl.ds(piece * 256, 256)
        partial[:, columns] = jnp.dot(
            normed[...], weights[:, :, columns].reshape(depth, 256), preferred_element_type=F32
        )


def spatial_kernel(here, tokens, partial, normed, mine, other, middle, out_ref, qkv, context, sems):
    core = here[2]
    outs = pl.ds(3 * INNER, INNER)
    copies = run(
        [
            pltpu.make_async_copy(mine.at[:, :, outs], out_ref.at[:, core], sems.at[0]),
            pltpu.make_async_copy(other.at[:, :, outs], out_ref.at[:, 1 - core], sems.at[1]),
        ]
    )
    depth = normed.shape[1]

    def product(columns):
        weight = other[:, :, columns].reshape(depth, 256)
        return partial[:, columns] + jnp.dot(normed[...], weight, preferred_element_type=F32)

    def store(columns, value):
        qkv[:, columns] = value.astype(BF16)

    project(product, store)
    for clip in range(tokens.shape[0] // ROWS):
        rows = pl.ds(clip * ROWS, ROWS)
        context[rows, :] = attend(qkv, rows, None).astype(BF16)
    wait(copies)
    parts, cores, twice, width = out_ref.shape
    half = twice // 2
    for side in range(2):
        columns = pl.ds(side * width, width)
        weight = out_ref[:, :, pl.ds(side * half, half)].reshape(parts * cores * half, width)
        added = jnp.dot(context[...], weight, preferred_element_type=F32)
        middle[:, columns] = (tokens[:, columns].astype(F32) + added).astype(BF16)


def place_kernel(here, *refs):
    pieces, placed, sems = refs[:-2], refs[-2], refs[-1]
    copies = []
    for side, piece in enumerate(pieces):
        target = placed.at[:, (here[1] + side // 2) % 2, (here[2] + side % 2) % 2]
        copies.append(pltpu.make_async_copy(piece, target, sems.at[side]))
    wait(run(copies))


def copy_kernel(source, target):
    target[...] = source[...]


def temporal_kernel(frames, middle, gain, placed, context, qkv):
    normed = norm_rows(middle[...].astype(F32), gain[...]).astype(BF16)
    rows, depth = middle.shape
    places = rows // frames

    def product(columns):
        weight = placed[:, :, :, :, columns].reshape(depth, 256)
        return jnp.dot(normed, weight, preferred_element_type=F32)

    def store(columns, value):
        split = value.reshape(frames, places, value.shape[1])
        for group in range(places // GROUP):
            own = split[:, group * GROUP : (group + 1) * GROUP].reshape(ROWS, value.shape[1])
            qkv[pl.ds(group * ROWS, ROWS), columns] = own.astype(BF16)

    project(product, store)
    place = lax.broadcasted_iota(jnp.int32, (ROWS, ROWS), 0) % GROUP
    same = place == lax.broadcasted_iota(jnp.int32, (ROWS, ROWS), 1) % GROUP
    outs = []
    for group in range(places // GROUP):
        out = attend(qkv, pl.ds(group * ROWS, ROWS), same)
        outs.append(out.reshape(frames, GROUP, INNER))
    context[...] = jnp.concatenate(outs, axis=1).reshape(rows, INNER).astype(BF16)


def kernel_call(body, kinds, out, operands, scratch=(), gflops=0, mib=4, room=24):
    near = pl.BlockSpec(memory_space=pltpu.VMEM)
    specs = {"s": pl.BlockSpec(memory_space=pltpu.SMEM), "v": near, "h": pl.BlockSpec(memory_space=pl.ANY)}
    return pl.pallas_call(
        body,
        out_shape=out,
        in_specs=[specs[kind] for kind in kinds],
        out_specs=jax.tree.map(lambda _: near, out),
        scratch_shapes=scratch,
        compiler_params=pltpu.CompilerParams(vmem_limit_bytes=room * MIB),
        cost_estimate=pl.CostEstimate(flops=int(gflops * 1e9), bytes_accessed=mib * MIB, transcendentals=0),
    )(*operands)


def moved(array, change):
    pairs = []
    for index in range(lax.axis_size("fsdp")):
        x, yl, core = change(index // 4, index // 2 % 2, index % 2)
        pairs.append((index, (x * 2 + yl) * 2 + core))
    return lax.ppermute(array, "fsdp", pairs)


def other_core(array):
    return moved(array, lambda x, yl, core: (x, yl, 1 - core))


def other_yl(array, beside):
    members, frames = lax.axis_size("fsdp"), lax.axis_size("tm")
    half = array.shape[0] // 2
    pieces = []
    for turn, piece in enumerate((array[:half], array[half:])):
        pairs = []
        for source in range(members * frames):
            member, frame = source // frames, source % frames
            pairs.append((source, (member ^ 2) * frames + (frame + turn * frames // 2) % frames))
        pieces.append(lax.ppermute(piece, ("fsdp", "tm"), pairs))
    *pieces, beside = lax.optimization_barrier((*pieces, beside))
    return jnp.concatenate(pieces, axis=0), beside


def along_x(shard):
    lines = [list(range(start, 16, 4)) for start in range(4)]
    return lax.all_gather(shard, "fsdp", axis_index_groups=lines)


def after(array, other):
    return lax.optimization_barrier((array, other))[0]


def shards(tokens, spatial_gain, spatial_qkv, spatial_out, temporal_gain, temporal_qkv, temporal_out):
    clips, _, places, depth = tokens.shape
    frames = lax.axis_size("tm")
    members = lax.axis_size("fsdp")
    parts, part = members // 2, depth // members
    rows = clips * places
    block = rows // frames
    flat = tokens.reshape(rows, depth)
    index = lax.axis_index("fsdp")
    here = jnp.stack([index // 4, index // 2 % 2, index % 2]).astype(jnp.int32)
    cores = [list(range(core, members, 2)) for core in range(2)]
    shape = jax.ShapeDtypeStruct

    def exchanged(array):
        sent = array.reshape(frames, block, array.shape[1])
        return lax.all_to_all(sent, "tm", split_axis=0, concat_axis=0, tiled=True).reshape(array.shape)

    def in_order(*pieces):
        return kernel_call(
            place_kernel,
            "s" + "h" * 4,
            shape((4, 2, 2, *pieces[0].shape[1:]), BF16),
            (here, *pieces),
            [pltpu.SemaphoreType.DMA((4,))],
        )

    packed = kernel_call(
        pack_kernel, "vv", shape((parts, part, 4 * INNER), BF16), (spatial_qkv, spatial_out), room=60
    )
    mine = lax.all_to_all(packed, "fsdp", 0, 0, axis_index_groups=cores, tiled=True)
    normed, normed_other = kernel_call(
        norm_kernel,
        "svv",
        [shape((rows, depth // 2), BF16)] * 2,
        (here, flat, spatial_gain.reshape(1, depth)),
        gflops=2,
        room=24,
    )
    partial = kernel_call(half_kernel, "vv", shape((rows, 3 * INNER), F32), (normed, mine), gflops=1, room=24)
    middle = kernel_call(
        spatial_kernel,
        "svvvvv",
        shape((rows, depth), BF16),
        (here, flat, partial, normed_other, mine, other_core(mine)),
        [
            pltpu.VMEM((parts, 2, part, INNER), BF16),
            pltpu.VMEM((rows, 3 * INNER), BF16),
            pltpu.VMEM((rows, INNER), BF16),
            pltpu.SemaphoreType.DMA((2,)),
        ],
        gflops=3,
        room=24,
    )
    shard, middle = lax.optimization_barrier((temporal_qkv, middle))
    arrived = exchanged(middle)
    own = along_x(shard)
    own_o = along_x(after(temporal_out, own))
    beside, own_o = other_yl(own, own_o)
    placed = in_order(own, other_core(own), beside, other_core(beside))
    arrived, own_o = lax.optimization_barrier((arrived, own_o))
    context = kernel_call(
        functools.partial(temporal_kernel, frames),
        "vvv",
        shape((rows, INNER), BF16),
        (arrived, temporal_gain.reshape(1, depth), placed),
        [pltpu.VMEM((rows, 3 * INNER), BF16)],
        gflops=4,
    )
    own, middle, context = lax.optimization_barrier((own_o, middle, context))
    returned = exchanged(context)
    beside = moved(own, lambda x, yl, core: (x, 1 - yl, core))
    swapped = other_core(jnp.stack([own, beside]))
    weight = in_order(own, swapped[0], beside, swapped[1]).reshape(INNER, depth)
    kept = kernel_call(copy_kernel, "v", shape((rows, depth), BF16), (middle,))
    encoded = kept.astype(F32) + jnp.dot(returned, weight, preferred_element_type=F32)
    return encoded.astype(BF16).reshape(tokens.shape)


def solution(mesh):
    placed = (
        P("fsdp", "tm", None, None),
        P(),
        P("fsdp", None),
        P("fsdp", None),
        P(),
        P("fsdp", None),
        P("fsdp", None),
    )
    return jax.shard_map(
        shards, mesh=mesh, in_specs=placed, out_specs=P("fsdp", "tm", None, None), check_vma=False
    )
```

```python
import functools

import jax
import jax.numpy as jnp
from jax import lax
from jax.experimental import pallas as pl
from jax.experimental.pallas import tpu as pltpu
from jax.sharding import PartitionSpec as P

HEAD = 64
HEADS = 8
INNER = 512
EPSILON = 1e-06
BF16, F32 = jnp.bfloat16, jnp.float32
GROUP = 8
PAIR = 2 * HEAD
ROWS = 256
MIB = 1 << 20


def norm_rows(values, gain):
    centre = values - jnp.mean(values, axis=-1, keepdims=True)
    spread = jnp.mean(centre * centre, axis=-1, keepdims=True)
    return centre * lax.rsqrt(spread + EPSILON) * gain


def attend(qkv, rows, same):
    low = lax.broadcasted_iota(jnp.int32, (ROWS, PAIR), 1) < HEAD
    outs = []
    for pair in range(HEADS // 2):
        queries = qkv[rows, pl.ds(pair * PAIR, PAIR)]
        keys = qkv[rows, pl.ds(INNER + pair * PAIR, PAIR)]
        values = qkv[rows, pl.ds(2 * INNER + pair * PAIR, PAIR)]
        values = jnp.concatenate([values, jnp.ones_like(values)], axis=1)
        halves = []
        for mine in (low, ~low):
            own = jnp.where(mine, queries, jnp.zeros_like(queries))
            scores = lax.dot_general(own, keys, (((1,), (1,)), ((), ())), preferred_element_type=F32)
            if same is not None:
                scores = jnp.where(same, scores, -1e30)
            exponent = jnp.exp(scores - jnp.max(scores, axis=-1, keepdims=True))
            summed = jnp.dot(exponent.astype(BF16), values, preferred_element_type=F32)
            halves.append(summed[:, :PAIR] / summed[:, PAIR:])
        outs.append(jnp.where(low, halves[0], halves[1]))
    return jnp.concatenate(outs, axis=1)


def project(product, store):
    for piece in range(3 * INNER // 256):
        columns = pl.ds(piece * 256, 256)
        value = product(columns)
        if piece < INNER // 256:
            value = value * HEAD**-0.5
        store(columns, value)


def pack_kernel(qkv, out, packed):
    depth, width = qkv.shape
    half = out.shape[1] // 2
    for index in range(packed.shape[0]):
        packed[index, :, pl.ds(0, width)] = qkv[...]
        packed[index, pl.ds(0, depth // 2), pl.ds(width, half)] = out[:, pl.ds(0, half)]
        packed[index, pl.ds(depth // 2, depth // 2), pl.ds(width, half)] = out[:, pl.ds(half, half)]


def run(copies):
    for copy in copies:
        copy.start()
    return copies


def wait(copies):
    for copy in copies:
        copy.wait()


def norm_kernel(here, tokens, gain, mine, other):
    normed = norm_rows(tokens[...].astype(F32), gain[...]).astype(BF16)
    depth, width = normed.shape[1], mine.shape[1]
    source = lax.broadcasted_iota(jnp.int32, (depth, width), 0)
    target = lax.broadcasted_iota(jnp.int32, (depth, width), 1)
    block = depth // 16
    first = target // block * (2 * block) + target % block
    for out, core in ((mine, here[2]), (other, 1 - here[2])):
        chosen = (source == first + core * block).astype(F32).astype(BF16)
        out[...] = jnp.dot(normed, chosen, preferred_element_type=F32).astype(BF16)


def half_kernel(normed, weights, partial):
    depth = normed.shape[1]
    for piece in range(partial.shape[1] // 256):
        columns = pl.ds(piece * 256, 256)
        partial[:, columns] = jnp.dot(
            normed[...], weights[:, :, columns].reshape(depth, 256), preferred_element_type=F32
        )


def spatial_kernel(here, tokens, partial, normed, mine, other, middle, out_ref, qkv, context, sems):
    core = here[2]
    outs = pl.ds(3 * INNER, INNER)
    copies = run(
        [
            pltpu.make_async_copy(mine.at[:, :, outs], out_ref.at[:, core], sems.at[0]),
            pltpu.make_async_copy(other.at[:, :, outs], out_ref.at[:, 1 - core], sems.at[1]),
        ]
    )
    depth = normed.shape[1]

    def product(columns):
        weight = other[:, :, columns].reshape(depth, 256)
        return partial[:, columns] + jnp.dot(normed[...], weight, preferred_element_type=F32)

    def store(columns, value):
        qkv[:, columns] = value.astype(BF16)

    project(product, store)
    for clip in range(tokens.shape[0] // ROWS):
        rows = pl.ds(clip * ROWS, ROWS)
        context[rows, :] = attend(qkv, rows, None).astype(BF16)
    wait(copies)
    parts, cores, twice, width = out_ref.shape
    half = twice // 2
    for side in range(2):
        columns = pl.ds(side * width, width)
        weight = out_ref[:, :, pl.ds(side * half, half)].reshape(parts * cores * half, width)
        added = jnp.dot(context[...], weight, preferred_element_type=F32)
        middle[:, columns] = (tokens[:, columns].astype(F32) + added).astype(BF16)


def place_kernel(here, *refs):
    pieces, placed, sems = refs[:-2], refs[-2], refs[-1]
    copies = []
    for side, piece in enumerate(pieces):
        target = placed.at[:, (here[1] + side // 2) % 2, (here[2] + side % 2) % 2]
        copies.append(pltpu.make_async_copy(piece, target, sems.at[side]))
    wait(run(copies))


def copy_kernel(source, target):
    target[...] = source[...]


def temporal_kernel(frames, middle, gain, placed, context, qkv):
    normed = norm_rows(middle[...].astype(F32), gain[...]).astype(BF16)
    rows, depth = middle.shape
    places = rows // frames

    def product(columns):
        weight = placed[:, :, :, :, columns].reshape(depth, 256)
        return jnp.dot(normed, weight, preferred_element_type=F32)

    def store(columns, value):
        split = value.reshape(frames, places, value.shape[1])
        for group in range(places // GROUP):
            own = split[:, group * GROUP : (group + 1) * GROUP].reshape(ROWS, value.shape[1])
            qkv[pl.ds(group * ROWS, ROWS), columns] = own.astype(BF16)

    project(product, store)
    place = lax.broadcasted_iota(jnp.int32, (ROWS, ROWS), 0) % GROUP
    same = place == lax.broadcasted_iota(jnp.int32, (ROWS, ROWS), 1) % GROUP
    outs = []
    for group in range(places // GROUP):
        out = attend(qkv, pl.ds(group * ROWS, ROWS), same)
        outs.append(out.reshape(frames, GROUP, INNER))
    context[...] = jnp.concatenate(outs, axis=1).reshape(rows, INNER).astype(BF16)


def kernel_call(body, kinds, out, operands, scratch=(), gflops=0, mib=4, room=24):
    near = pl.BlockSpec(memory_space=pltpu.VMEM)
    specs = {"s": pl.BlockSpec(memory_space=pltpu.SMEM), "v": near, "h": pl.BlockSpec(memory_space=pl.ANY)}
    return pl.pallas_call(
        body,
        out_shape=out,
        in_specs=[specs[kind] for kind in kinds],
        out_specs=jax.tree.map(lambda _: near, out),
        scratch_shapes=scratch,
        compiler_params=pltpu.CompilerParams(vmem_limit_bytes=room * MIB),
        cost_estimate=pl.CostEstimate(flops=int(gflops * 1e9), bytes_accessed=mib * MIB, transcendentals=0),
    )(*operands)


def moved(array, change):
    pairs = []
    for index in range(lax.axis_size("fsdp")):
        x, yl, core = change(index // 4, index // 2 % 2, index % 2)
        pairs.append((index, (x * 2 + yl) * 2 + core))
    return lax.ppermute(array, "fsdp", pairs)


def other_core(array):
    return moved(array, lambda x, yl, core: (x, yl, 1 - core))


def other_yl(array, beside):
    members, frames = lax.axis_size("fsdp"), lax.axis_size("tm")
    half = array.shape[0] // 2
    pieces = []
    for turn, piece in enumerate((array[:half], array[half:])):
        pairs = []
        for source in range(members * frames):
            member, frame = source // frames, source % frames
            pairs.append((source, (member ^ 2) * frames + (frame + turn * frames // 2) % frames))
        pieces.append(lax.ppermute(piece, ("fsdp", "tm"), pairs))
    *pieces, beside = lax.optimization_barrier((*pieces, beside))
    return jnp.concatenate(pieces, axis=0), beside


def along_x(shard):
    lines = [list(range(start, 16, 4)) for start in range(4)]
    return lax.all_gather(shard, "fsdp", axis_index_groups=lines)


def after(array, other):
    return lax.optimization_barrier((array, other))[0]


def shards(tokens, spatial_gain, spatial_qkv, spatial_out, temporal_gain, temporal_qkv, temporal_out):
    clips, _, places, depth = tokens.shape
    frames = lax.axis_size("tm")
    members = lax.axis_size("fsdp")
    parts, part = members // 2, depth // members
    rows = clips * places
    block = rows // frames
    flat = tokens.reshape(rows, depth)
    index = lax.axis_index("fsdp")
    here = jnp.stack([index // 4, index // 2 % 2, index % 2]).astype(jnp.int32)
    cores = [list(range(core, members, 2)) for core in range(2)]
    shape = jax.ShapeDtypeStruct

    def exchanged(array):
        sent = array.reshape(frames, block, array.shape[1])
        return lax.all_to_all(sent, "tm", split_axis=0, concat_axis=0, tiled=True).reshape(array.shape)

    def in_order(*pieces):
        return kernel_call(
            place_kernel,
            "s" + "h" * 4,
            shape((4, 2, 2, *pieces[0].shape[1:]), BF16),
            (here, *pieces),
            [pltpu.SemaphoreType.DMA((4,))],
        )

    packed = kernel_call(
        pack_kernel, "vv", shape((parts, part, 4 * INNER), BF16), (spatial_qkv, spatial_out), room=60
    )
    mine = lax.all_to_all(packed, "fsdp", 0, 0, axis_index_groups=cores, tiled=True)
    normed, normed_other = kernel_call(
        norm_kernel,
        "svv",
        [shape((rows, depth // 2), BF16)] * 2,
        (here, flat, spatial_gain.reshape(1, depth)),
        gflops=2,
        room=24,
    )
    partial = kernel_call(half_kernel, "vv", shape((rows, 3 * INNER), F32), (normed, mine), gflops=1, room=24)
    middle = kernel_call(
        spatial_kernel,
        "svvvvv",
        shape((rows, depth), BF16),
        (here, flat, partial, normed_other, mine, other_core(mine)),
        [
            pltpu.VMEM((parts, 2, part, INNER), BF16),
            pltpu.VMEM((rows, 3 * INNER), BF16),
            pltpu.VMEM((rows, INNER), BF16),
            pltpu.SemaphoreType.DMA((2,)),
        ],
        gflops=3,
        room=24,
    )
    shard, middle = lax.optimization_barrier((temporal_qkv, middle))
    arrived = exchanged(middle)
    own = along_x(shard)
    own_o = along_x(after(temporal_out, own))
    beside, own_o = other_yl(own, own_o)
    placed = in_order(own, other_core(own), beside, other_core(beside))
    arrived, own_o = lax.optimization_barrier((arrived, own_o))
    context = kernel_call(
        functools.partial(temporal_kernel, frames),
        "vvv",
        shape((rows, INNER), BF16),
        (arrived, temporal_gain.reshape(1, depth), placed),
        [pltpu.VMEM((rows, 3 * INNER), BF16)],
        gflops=4,
    )
    own, middle, context = lax.optimization_barrier((own_o, middle, context))
    returned = exchanged(context)
    beside = moved(own, lambda x, yl, core: (x, 1 - yl, core))
    swapped = other_core(jnp.stack([own, beside]))
    weight = in_order(own, swapped[0], beside, swapped[1]).reshape(INNER, depth)
    kept = kernel_call(copy_kernel, "v", shape((rows, depth), BF16), (middle,))
    encoded = kept.astype(F32) + jnp.dot(returned, weight, preferred_element_type=F32)
    return encoded.astype(BF16).reshape(tokens.shape)


def solution(mesh):
    placed = (
        P("fsdp", "tm", None, None),
        P(),
        P("fsdp", None),
        P("fsdp", None),
        P(),
        P("fsdp", None),
        P("fsdp", None),
    )
    return jax.shard_map(
        shards, mesh=mesh, in_specs=placed, out_specs=P("fsdp", "tm", None, None), check_vma=False
    )
```

```python
import functools

import jax
import jax.numpy as jnp
from jax import lax
from jax.experimental import pallas as pl
from jax.experimental.pallas import tpu as pltpu
from jax.sharding import PartitionSpec as P

HEAD = 64
HEADS = 8
INNER = 512
EPSILON = 1e-06
LOG2_E = 1.4426950408889634
BF16, F32 = jnp.bfloat16, jnp.float32
GROUP = 8
PAIR = 2 * HEAD
ROWS = 256
MIB = 1 << 20


def norm_rows(values, gain):
    centre = values - jnp.mean(values, axis=-1, keepdims=True)
    spread = jnp.mean(centre * centre, axis=-1, keepdims=True)
    return centre * lax.rsqrt(spread + EPSILON) * gain


def attend(qkv, rows, same):
    low = lax.broadcasted_iota(jnp.int32, (ROWS, PAIR), 1) < HEAD
    outs = []
    for pair in range(HEADS // 2):
        queries = qkv[rows, pl.ds(pair * PAIR, PAIR)]
        keys = qkv[rows, pl.ds(INNER + pair * PAIR, PAIR)]
        values = qkv[rows, pl.ds(2 * INNER + pair * PAIR, PAIR)]
        values = jnp.concatenate([values, jnp.ones_like(values)], axis=1)
        halves = []
        for mine in (low, ~low):
            own = jnp.where(mine, queries, jnp.zeros_like(queries))
            scores = lax.dot_general(own, keys, (((1,), (1,)), ((), ())), preferred_element_type=F32)
            if same is not None:
                scores = jnp.where(same, scores, -1e30)
            exponent = jnp.exp2(scores - jnp.max(scores, axis=-1, keepdims=True))
            summed = jnp.dot(exponent.astype(BF16), values, preferred_element_type=F32)
            halves.append(summed[:, :PAIR] / summed[:, PAIR:])
        outs.append(jnp.where(low, halves[0], halves[1]))
    return jnp.concatenate(outs, axis=1)


def project(product, store):
    for piece in range(3 * INNER // 256):
        columns = pl.ds(piece * 256, 256)
        value = product(columns)
        if piece < INNER // 256:
            value = value * (HEAD**-0.5 * LOG2_E)
        store(columns, value)


def pack_kernel(qkv, out, packed, joined, sems):
    depth, width = qkv.shape
    half = out.shape[1] // 2
    joined[:, pl.ds(0, width)] = qkv[...]
    joined[pl.ds(0, depth // 2), pl.ds(width, half)] = out[:, pl.ds(0, half)]
    joined[pl.ds(depth // 2, depth // 2), pl.ds(width, half)] = out[:, pl.ds(half, half)]
    wait(run([pltpu.make_async_copy(joined, packed.at[index], sems.at[index]) for index in range(packed.shape[0])]))


def run(copies):
    for copy in copies:
        copy.start()
    return copies


def wait(copies):
    for copy in copies:
        copy.wait()


def norm_kernel(here, tokens, gain, mine, other):
    normed = norm_rows(tokens[...].astype(F32), gain[...]).astype(BF16)
    depth, width = normed.shape[1], mine.shape[1]
    source = lax.broadcasted_iota(jnp.int32, (depth, width), 0)
    target = lax.broadcasted_iota(jnp.int32, (depth, width), 1)
    block = depth // 16
    first = target // block * (2 * block) + target % block
    for out, core in ((mine, here[2]), (other, 1 - here[2])):
        chosen = (source == first + core * block).astype(F32).astype(BF16)
        out[...] = jnp.dot(normed, chosen, preferred_element_type=F32).astype(BF16)


def half_kernel(normed, weights, partial):
    depth = normed.shape[1]
    for piece in range(partial.shape[1] // 256):
        columns = pl.ds(piece * 256, 256)
        partial[:, columns] = jnp.dot(
            normed[...], weights[:, :, columns].reshape(depth, 256), preferred_element_type=F32
        )


def spatial_kernel(here, tokens, partial, normed, mine, other, middle, out_ref, qkv, context, sems):
    core = here[2]
    outs = pl.ds(3 * INNER, INNER)
    copies = run(
        [
            pltpu.make_async_copy(mine.at[:, :, outs], out_ref.at[:, core], sems.at[0]),
            pltpu.make_async_copy(other.at[:, :, outs], out_ref.at[:, 1 - core], sems.at[1]),
        ]
    )
    depth = normed.shape[1]

    def product(columns):
        weight = other[:, :, columns].reshape(depth, 256)
        return partial[:, columns] + jnp.dot(normed[...], weight, preferred_element_type=F32)

    def store(columns, value):
        qkv[:, columns] = value.astype(BF16)

    project(product, store)
    for clip in range(tokens.shape[0] // ROWS):
        rows = pl.ds(clip * ROWS, ROWS)
        context[rows, :] = attend(qkv, rows, None).astype(BF16)
    wait(copies)
    parts, cores, twice, width = out_ref.shape
    half = twice // 2
    for side in range(2):
        columns = pl.ds(side * width, width)
        weight = out_ref[:, :, pl.ds(side * half, half)].reshape(parts * cores * half, width)
        added = jnp.dot(context[...], weight, preferred_element_type=F32)
        middle[:, columns] = (tokens[:, columns].astype(F32) + added).astype(BF16)


def place_kernel(here, *refs):
    pieces, placed, sems = refs[:-2], refs[-2], refs[-1]
    copies = []
    for side, piece in enumerate(pieces):
        target = placed.at[:, (here[1] + side // 2) % 2, (here[2] + side % 2) % 2]
        copies.append(pltpu.make_async_copy(piece, target, sems.at[side]))
    wait(run(copies))


def copy_kernel(source, target):
    target[...] = source[...]


def temporal_kernel(frames, middle, gain, placed, context, qkv):
    normed = norm_rows(middle[...].astype(F32), gain[...]).astype(BF16)
    rows, depth = middle.shape
    places = rows // frames

    def product(columns):
        weight = placed[:, :, :, :, columns].reshape(depth, 256)
        return jnp.dot(normed, weight, preferred_element_type=F32)

    def store(columns, value):
        split = value.reshape(frames, places, value.shape[1])
        for group in range(places // GROUP):
            own = split[:, group * GROUP : (group + 1) * GROUP].reshape(ROWS, value.shape[1])
            qkv[pl.ds(group * ROWS, ROWS), columns] = own.astype(BF16)

    project(product, store)
    place = lax.broadcasted_iota(jnp.int32, (ROWS, ROWS), 0) % GROUP
    same = place == lax.broadcasted_iota(jnp.int32, (ROWS, ROWS), 1) % GROUP
    outs = []
    for group in range(places // GROUP):
        out = attend(qkv, pl.ds(group * ROWS, ROWS), same)
        outs.append(out.reshape(frames, GROUP, INNER))
    context[...] = jnp.concatenate(outs, axis=1).reshape(rows, INNER).astype(BF16)


def kernel_call(body, kinds, out, operands, scratch=(), gflops=0, mib=4, room=24, away=pltpu.VMEM):
    near = pl.BlockSpec(memory_space=pltpu.VMEM)
    specs = {"s": pl.BlockSpec(memory_space=pltpu.SMEM), "v": near, "h": pl.BlockSpec(memory_space=pl.ANY)}
    return pl.pallas_call(
        body,
        out_shape=out,
        in_specs=[specs[kind] for kind in kinds],
        out_specs=jax.tree.map(lambda _: pl.BlockSpec(memory_space=away), out),
        scratch_shapes=scratch,
        compiler_params=pltpu.CompilerParams(vmem_limit_bytes=room * MIB),
        cost_estimate=pl.CostEstimate(flops=int(gflops * 1e9), bytes_accessed=mib * MIB, transcendentals=0),
    )(*operands)


def moved(array, change):
    pairs = []
    for index in range(lax.axis_size("fsdp")):
        x, yl, core = change(index // 4, index // 2 % 2, index % 2)
        pairs.append((index, (x * 2 + yl) * 2 + core))
    return lax.ppermute(array, "fsdp", pairs)


def other_core(array):
    return moved(array, lambda x, yl, core: (x, yl, 1 - core))


def other_yl(array, beside):
    members, frames = lax.axis_size("fsdp"), lax.axis_size("tm")
    half = array.shape[0] // 2
    pieces = []
    for turn, piece in enumerate((array[:half], array[half:])):
        pairs = []
        for source in range(members * frames):
            member, frame = source // frames, source % frames
            pairs.append((source, (member ^ 2) * frames + (frame + turn * frames // 2) % frames))
        pieces.append(lax.ppermute(piece, ("fsdp", "tm"), pairs))
    *pieces, beside = lax.optimization_barrier((*pieces, beside))
    return jnp.concatenate(pieces, axis=0), beside


def along_x(shard):
    lines = [list(range(start, 16, 4)) for start in range(4)]
    return lax.all_gather(shard, "fsdp", axis_index_groups=lines)


def after(array, other):
    return lax.optimization_barrier((array, other))[0]


def shards(tokens, spatial_gain, spatial_qkv, spatial_out, temporal_gain, temporal_qkv, temporal_out):
    clips, _, places, depth = tokens.shape
    frames = lax.axis_size("tm")
    members = lax.axis_size("fsdp")
    parts, part = members // 2, depth // members
    rows = clips * places
    block = rows // frames
    flat = tokens.reshape(rows, depth)
    index = lax.axis_index("fsdp")
    here = jnp.stack([index // 4, index // 2 % 2, index % 2]).astype(jnp.int32)
    cores = [list(range(core, members, 2)) for core in range(2)]
    shape = jax.ShapeDtypeStruct

    def exchanged(array):
        sent = array.reshape(frames, block, array.shape[1])
        return lax.all_to_all(sent, "tm", split_axis=0, concat_axis=0, tiled=True).reshape(array.shape)

    def in_order(*pieces):
        return kernel_call(
            place_kernel,
            "s" + "h" * 4,
            shape((4, 2, 2, *pieces[0].shape[1:]), BF16),
            (here, *pieces),
            [pltpu.SemaphoreType.DMA((4,))],
        )

    packed = kernel_call(
        pack_kernel,
        "vv",
        shape((parts, part, 4 * INNER), BF16),
        (spatial_qkv, spatial_out),
        [pltpu.VMEM((part, 4 * INNER), BF16), pltpu.SemaphoreType.DMA((parts,))],
        room=60,
        away=pl.ANY,
    )
    mine = lax.all_to_all(packed, "fsdp", 0, 0, axis_index_groups=cores, tiled=True)
    normed, normed_other = kernel_call(
        norm_kernel,
        "svv",
        [shape((rows, depth // 2), BF16)] * 2,
        (here, flat, spatial_gain.reshape(1, depth)),
        gflops=2,
        room=24,
    )
    partial = kernel_call(half_kernel, "vv", shape((rows, 3 * INNER), F32), (normed, mine), gflops=1, room=24)
    middle = kernel_call(
        spatial_kernel,
        "svvvvv",
        shape((rows, depth), BF16),
        (here, flat, partial, normed_other, mine, other_core(mine)),
        [
            pltpu.VMEM((parts, 2, part, INNER), BF16),
            pltpu.VMEM((rows, 3 * INNER), BF16),
            pltpu.VMEM((rows, INNER), BF16),
            pltpu.SemaphoreType.DMA((2,)),
        ],
        gflops=3,
        room=24,
    )
    shard, middle = lax.optimization_barrier((temporal_qkv, middle))
    arrived = exchanged(middle)
    own = along_x(shard)
    own_o = along_x(after(temporal_out, own))
    beside, own_o = other_yl(own, own_o)
    placed = in_order(own, other_core(own), beside, other_core(beside))
    arrived, own_o = lax.optimization_barrier((arrived, own_o))
    context = kernel_call(
        functools.partial(temporal_kernel, frames),
        "vvv",
        shape((rows, INNER), BF16),
        (arrived, temporal_gain.reshape(1, depth), placed),
        [pltpu.VMEM((rows, 3 * INNER), BF16)],
        gflops=4,
    )
    own, middle, context = lax.optimization_barrier((own_o, middle, context))
    returned = exchanged(context)
    beside = moved(own, lambda x, yl, core: (x, 1 - yl, core))
    swapped = other_core(jnp.stack([own, beside]))
    weight = in_order(own, swapped[0], beside, swapped[1]).reshape(INNER, depth)
    kept = kernel_call(copy_kernel, "v", shape((rows, depth), BF16), (middle,))
    encoded = kept.astype(F32) + jnp.dot(returned, weight, preferred_element_type=F32)
    return encoded.astype(BF16).reshape(tokens.shape)


def solution(mesh):
    placed = (
        P("fsdp", "tm", None, None),
        P(),
        P("fsdp", None),
        P("fsdp", None),
        P(),
        P("fsdp", None),
        P("fsdp", None),
    )
    return jax.shard_map(
        shards, mesh=mesh, in_specs=placed, out_specs=P("fsdp", "tm", None, None), check_vma=False
    )
```

```python
import functools

import jax
import jax.numpy as jnp
from jax import lax
from jax.experimental import pallas as pl
from jax.experimental.pallas import tpu as pltpu
from jax.sharding import PartitionSpec as P

HEAD = 64
HEADS = 8
INNER = 512
EPSILON = 1e-06
BF16, F32 = jnp.bfloat16, jnp.float32
GROUP = 8
PAIR = 2 * HEAD
ROWS = 256
MIB = 1 << 20


def norm_rows(values, gain):
    centre = values - jnp.mean(values, axis=-1, keepdims=True)
    spread = jnp.mean(centre * centre, axis=-1, keepdims=True)
    return centre * lax.rsqrt(spread + EPSILON) * gain


def attend(qkv, rows, same):
    low = lax.broadcasted_iota(jnp.int32, (ROWS, PAIR), 1) < HEAD
    outs = []
    for pair in range(HEADS // 2):
        queries = qkv[rows, pl.ds(pair * PAIR, PAIR)]
        keys = qkv[rows, pl.ds(INNER + pair * PAIR, PAIR)]
        values = qkv[rows, pl.ds(2 * INNER + pair * PAIR, PAIR)]
        values = jnp.concatenate([values, jnp.ones_like(values)], axis=1)
        halves = []
        for mine in (low, ~low):
            own = jnp.where(mine, queries, jnp.zeros_like(queries))
            scores = lax.dot_general(own, keys, (((1,), (1,)), ((), ())), preferred_element_type=F32)
            if same is not None:
                scores = jnp.where(same, scores, -1e30)
            exponent = jnp.exp(scores - jnp.max(scores, axis=-1, keepdims=True))
            summed = jnp.dot(exponent.astype(BF16), values, preferred_element_type=F32)
            halves.append(summed[:, :PAIR] / summed[:, PAIR:])
        outs.append(jnp.where(low, halves[0], halves[1]))
    return jnp.concatenate(outs, axis=1)


def project(product, store):
    for piece in range(3 * INNER // 256):
        columns = pl.ds(piece * 256, 256)
        value = product(columns)
        if piece < INNER // 256:
            value = value * HEAD**-0.5
        store(columns, value)


def pack_kernel(qkv, out, packed):
    depth, width = qkv.shape
    half = out.shape[1] // 2
    for index in range(packed.shape[0]):
        packed[index, :, pl.ds(0, width)] = qkv[...]
        packed[index, pl.ds(0, depth // 2), pl.ds(width, half)] = out[:, pl.ds(0, half)]
        packed[index, pl.ds(depth // 2, depth // 2), pl.ds(width, half)] = out[:, pl.ds(half, half)]


def run(copies):
    for copy in copies:
        copy.start()
    return copies


def wait(copies):
    for copy in copies:
        copy.wait()


def half_kernel(here, tokens, gain, weights, partial, other):
    normed = norm_rows(tokens[...].astype(F32), gain[...]).astype(BF16)
    depth, width = normed.shape[1], other.shape[1]
    source = lax.broadcasted_iota(jnp.int32, (depth, width), 0)
    target = lax.broadcasted_iota(jnp.int32, (depth, width), 1)
    block = depth // 16
    first = target // block * (2 * block) + target % block

    def columns_of(core):
        chosen = (source == first + core * block).astype(F32).astype(BF16)
        return jnp.dot(normed, chosen, preferred_element_type=F32).astype(BF16)

    other[...] = columns_of(1 - here[2])
    mine = columns_of(here[2])
    for piece in range(partial.shape[1] // 256):
        columns = pl.ds(piece * 256, 256)
        weight = weights[:, :, columns].reshape(width, 256)
        partial[:, columns] = jnp.dot(mine, weight, preferred_element_type=F32)


def spatial_kernel(here, tokens, partial, normed, mine, other, middle, out_ref, qkv, context, sems):
    core = here[2]
    outs = pl.ds(3 * INNER, INNER)
    copies = run(
        [
            pltpu.make_async_copy(mine.at[:, :, outs], out_ref.at[:, core], sems.at[0]),
            pltpu.make_async_copy(other.at[:, :, outs], out_ref.at[:, 1 - core], sems.at[1]),
        ]
    )
    depth = normed.shape[1]

    def product(columns):
        weight = other[:, :, columns].reshape(depth, 256)
        return partial[:, columns] + jnp.dot(normed[...], weight, preferred_element_type=F32)

    def store(columns, value):
        qkv[:, columns] = value.astype(BF16)

    project(product, store)
    for clip in range(tokens.shape[0] // ROWS):
        rows = pl.ds(clip * ROWS, ROWS)
        context[rows, :] = attend(qkv, rows, None).astype(BF16)
    wait(copies)
    parts, cores, twice, width = out_ref.shape
    half = twice // 2
    for side in range(2):
        columns = pl.ds(side * width, width)
        weight = out_ref[:, :, pl.ds(side * half, half)].reshape(parts * cores * half, width)
        added = jnp.dot(context[...], weight, preferred_element_type=F32)
        middle[:, columns] = (tokens[:, columns].astype(F32) + added).astype(BF16)


def place_kernel(here, *refs):
    pieces, placed, sems = refs[:-2], refs[-2], refs[-1]
    copies = []
    for side, piece in enumerate(pieces):
        target = placed.at[:, (here[1] + side // 2) % 2, (here[2] + side % 2) % 2]
        copies.append(pltpu.make_async_copy(piece, target, sems.at[side]))
    wait(run(copies))


def copy_kernel(source, target):
    target[...] = source[...]


def temporal_kernel(frames, middle, gain, placed, context, qkv):
    normed = norm_rows(middle[...].astype(F32), gain[...]).astype(BF16)
    rows, depth = middle.shape
    places = rows // frames

    def product(columns):
        weight = placed[:, :, :, :, columns].reshape(depth, 256)
        return jnp.dot(normed, weight, preferred_element_type=F32)

    def store(columns, value):
        split = value.reshape(frames, places, value.shape[1])
        for group in range(places // GROUP):
            own = split[:, group * GROUP : (group + 1) * GROUP].reshape(ROWS, value.shape[1])
            qkv[pl.ds(group * ROWS, ROWS), columns] = own.astype(BF16)

    project(product, store)
    place = lax.broadcasted_iota(jnp.int32, (ROWS, ROWS), 0) % GROUP
    same = place == lax.broadcasted_iota(jnp.int32, (ROWS, ROWS), 1) % GROUP
    outs = []
    for group in range(places // GROUP):
        out = attend(qkv, pl.ds(group * ROWS, ROWS), same)
        outs.append(out.reshape(frames, GROUP, INNER))
    context[...] = jnp.concatenate(outs, axis=1).reshape(rows, INNER).astype(BF16)


def kernel_call(body, kinds, out, operands, scratch=(), gflops=0, mib=4, room=24):
    near = pl.BlockSpec(memory_space=pltpu.VMEM)
    specs = {"s": pl.BlockSpec(memory_space=pltpu.SMEM), "v": near, "h": pl.BlockSpec(memory_space=pl.ANY)}
    return pl.pallas_call(
        body,
        out_shape=out,
        in_specs=[specs[kind] for kind in kinds],
        out_specs=jax.tree.map(lambda _: near, out),
        scratch_shapes=scratch,
        compiler_params=pltpu.CompilerParams(vmem_limit_bytes=room * MIB),
        cost_estimate=pl.CostEstimate(flops=int(gflops * 1e9), bytes_accessed=mib * MIB, transcendentals=0),
    )(*operands)


def moved(array, change):
    pairs = []
    for index in range(lax.axis_size("fsdp")):
        x, yl, core = change(index // 4, index // 2 % 2, index % 2)
        pairs.append((index, (x * 2 + yl) * 2 + core))
    return lax.ppermute(array, "fsdp", pairs)


def other_core(array):
    return moved(array, lambda x, yl, core: (x, yl, 1 - core))


def other_yl(array, beside):
    members, frames = lax.axis_size("fsdp"), lax.axis_size("tm")
    half = array.shape[0] // 2
    pieces = []
    for turn, piece in enumerate((array[:half], array[half:])):
        pairs = []
        for source in range(members * frames):
            member, frame = source // frames, source % frames
            pairs.append((source, (member ^ 2) * frames + (frame + turn * frames // 2) % frames))
        pieces.append(lax.ppermute(piece, ("fsdp", "tm"), pairs))
    *pieces, beside = lax.optimization_barrier((*pieces, beside))
    return jnp.concatenate(pieces, axis=0), beside


def along_x(shard):
    lines = [list(range(start, 16, 4)) for start in range(4)]
    return lax.all_gather(shard, "fsdp", axis_index_groups=lines)


def after(array, other):
    return lax.optimization_barrier((array, other))[0]


def shards(tokens, spatial_gain, spatial_qkv, spatial_out, temporal_gain, temporal_qkv, temporal_out):
    clips, _, places, depth = tokens.shape
    frames = lax.axis_size("tm")
    members = lax.axis_size("fsdp")
    parts, part = members // 2, depth // members
    rows = clips * places
    block = rows // frames
    flat = tokens.reshape(rows, depth)
    index = lax.axis_index("fsdp")
    here = jnp.stack([index // 4, index // 2 % 2, index % 2]).astype(jnp.int32)
    cores = [list(range(core, members, 2)) for core in range(2)]
    shape = jax.ShapeDtypeStruct

    def exchanged(array):
        sent = array.reshape(frames, block, array.shape[1])
        return lax.all_to_all(sent, "tm", split_axis=0, concat_axis=0, tiled=True).reshape(array.shape)

    def in_order(*pieces):
        return kernel_call(
            place_kernel,
            "s" + "h" * 4,
            shape((4, 2, 2, *pieces[0].shape[1:]), BF16),
            (here, *pieces),
            [pltpu.SemaphoreType.DMA((4,))],
        )

    packed = kernel_call(
        pack_kernel, "vv", shape((parts, part, 4 * INNER), BF16), (spatial_qkv, spatial_out), room=60
    )
    mine = lax.all_to_all(packed, "fsdp", 0, 0, axis_index_groups=cores, tiled=True)
    partial, normed_other = kernel_call(
        half_kernel,
        "svvv",
        [shape((rows, 3 * INNER), F32), shape((rows, depth // 2), BF16)],
        (here, flat, spatial_gain.reshape(1, depth), mine),
        gflops=3,
    )
    middle = kernel_call(
        spatial_kernel,
        "svvvvv",
        shape((rows, depth), BF16),
        (here, flat, partial, normed_other, mine, other_core(mine)),
        [
            pltpu.VMEM((parts, 2, part, INNER), BF16),
            pltpu.VMEM((rows, 3 * INNER), BF16),
            pltpu.VMEM((rows, INNER), BF16),
            pltpu.SemaphoreType.DMA((2,)),
        ],
        gflops=3,
        room=24,
    )
    shard, middle = lax.optimization_barrier((temporal_qkv, middle))
    arrived = exchanged(middle)
    own = along_x(shard)
    own_o = along_x(after(temporal_out, own))
    beside, own_o = other_yl(own, own_o)
    placed = in_order(own, other_core(own), beside, other_core(beside))
    arrived, own_o = lax.optimization_barrier((arrived, own_o))
    context = kernel_call(
        functools.partial(temporal_kernel, frames),
        "vvv",
        shape((rows, INNER), BF16),
        (arrived, temporal_gain.reshape(1, depth), placed),
        [pltpu.VMEM((rows, 3 * INNER), BF16)],
        gflops=4,
    )
    own, middle, context = lax.optimization_barrier((own_o, middle, context))
    returned = exchanged(context)
    beside = moved(own, lambda x, yl, core: (x, 1 - yl, core))
    swapped = other_core(jnp.stack([own, beside]))
    weight = in_order(own, swapped[0], beside, swapped[1]).reshape(INNER, depth)
    kept = kernel_call(copy_kernel, "v", shape((rows, depth), BF16), (middle,))
    encoded = kept.astype(F32) + jnp.dot(returned, weight, preferred_element_type=F32)
    return encoded.astype(BF16).reshape(tokens.shape)


def solution(mesh):
    placed = (
        P("fsdp", "tm", None, None),
        P(),
        P("fsdp", None),
        P("fsdp", None),
        P(),
        P("fsdp", None),
        P("fsdp", None),
    )
    return jax.shard_map(
        shards, mesh=mesh, in_specs=placed, out_specs=P("fsdp", "tm", None, None), check_vma=False
    )
```
